32 devices in a mesh: slides: 2 (over x), tok: 16 (over z, y, core).
Axes of the slice: x: 2, y: 2, z: 4, core: 2. Of those that a mesh axis runs over, the one named last changes fastest.
Arguments:
- queries: bfloat16 [8, 2048, 768], P('slides', 'tok'), parts along dimension 0, may hold values from -7 to 7
- key_rows: bfloat16 [8, 2048, 768], P('slides', 'tok'), parts along dimension 0, may hold values from -6 to 6
- value_rows: bfloat16 [8, 2048, 768], P('slides', 'tok'), parts along dimension 0, may hold values from -6 to 6
- projected_output_gradient: bfloat16 [8, 32768, 768], P('slides', 'tok'), parts along dimension 0, may hold values from -24 to 24
- out_weight: bfloat16 [768, 768], replicated, may hold values from -0.21875 to 0.21875
- offsets: int32 [16], replicated, may hold values from 0 to 15, each once
Outputs:
- grad_queries: bfloat16 [8, 2048, 768], P('slides', 'tok'), parts along dimension 0
- grad_keys: bfloat16 [8, 2048, 768], P('slides', 'tok'), parts along dimension 0
- grad_values: bfloat16 [8, 2048, 768], P('slides', 'tok'), parts along dimension 0
- grad_weight: float32 [1536, 768], P(('slides', 'tok')), parts along dimension 0
The draws below stay inside these ranges and needn't reach their ends.
There are 2 independent parts, one for each index of `slides`. The reference program is written for one: setup_inputs(seed, part) draws one part's arguments, and reference() takes and returns one part's arrays. A program takes and returns all parts, laid end to end along the dimension named above; an argument that names none is the same for every part. Nothing has to cross between parts.
Inputs may be any that keep to these rules, and one draw needn't show every extreme that they name: offsets names each of the 16 phases once.
All inputs are finite; a program needn't handle non-finite values.
Results may differ from the reference program's by a relative error of at most 0.014.
Values may be sent and summed in bfloat16 or wider, within the bound.
A program may use at most 192 MiB of HBM per device.

```python
import jax
import jax.numpy as jnp
from jax import lax

D = 768
HEADS = 16
DILATION_RATE = 16
ROUNDS = 4
ROWS = 2048
TOKENS = 32768
N_TOK = 16


def draw_queries(key, part):
    shape_all = (ROUNDS, ROWS, D)
    drawn = jnp.clip(jax.random.normal(jax.random.fold_in(key, 11), shape_all, jnp.float32), -5.0, 5.0)
    return drawn.astype(jnp.bfloat16)


def draw_key_rows(key, part):
    shape_all = (ROUNDS, ROWS, D)
    drawn = jnp.clip(jax.random.normal(jax.random.fold_in(key, 21), shape_all, jnp.float32), -5.0, 5.0)
    return drawn.astype(jnp.bfloat16)


def raised(values, stream_key, source, target, parts, factor):
    owner, partner = [(jnp.arange(values.shape[dim]) // (values.shape[dim] // parts)).reshape([-1 if axis == dim else 1 for axis in range(values.ndim)]) for dim in (source, target)]
    chosen = jax.random.permutation(stream_key, parts)[partner]
    strong = (owner == chosen) | (owner == (partner + parts // 2) % parts)
    return jnp.where(strong, factor * values, values)


def block_levels(own_key, shape, shards, least, top_value):
    factor_of, own = 1.0, jax.random.fold_in(own_key, 6)
    for dim, parts in shards:
        steps = jnp.exp(jax.random.uniform(jax.random.fold_in(own, dim), (parts,), jnp.float32, least / len(shards), top_value / len(shards)))
        factor_of = factor_of * jnp.repeat(steps, shape[dim] // parts).reshape([-1 if axis == dim else 1 for axis in range(len(shape))])
    return factor_of


def scatter_about(key, shape, scale, most, shards=(), kind=jnp.bfloat16):
    values = scale * jax.random.normal(key, shape, jnp.float32)
    if shards:
        values = values * block_levels(key, shape, shards, -0.22, 0.18)
    return jnp.clip(values, -most, most).astype(kind)


def heavy_noise(stream_key, shape, scale, bound, pieces, heavy, kind=jnp.bfloat16):
    values = scale * jax.random.normal(stream_key, shape, jnp.float32)
    if pieces:
        values = values * block_levels(stream_key, shape, pieces, -0.22, 0.18)
    return jnp.clip(raised(values, jax.random.fold_in(stream_key, 3), *heavy), -bound, bound).astype(kind)


def setup_inputs(seed: int = 0, part: int = 0) -> dict:
    key_of = jax.random.split(jax.random.key(seed), 7)
    part_keys = jax.random.split(jax.random.fold_in(key_of[6], part), 7)
    return {
        "queries": draw_queries(jax.random.fold_in(jax.random.fold_in(key_of[6], part), 71), part),
        "key_rows": draw_key_rows(jax.random.fold_in(jax.random.fold_in(key_of[6], part), 71), part),
        "value_rows": scatter_about(part_keys[2], (ROUNDS, ROWS, D), 1.0, 6.0, ((1, 16),)),
        "projected_output_gradient": heavy_noise(part_keys[3], (ROUNDS, TOKENS, D), 4.0, 24.0, ((1, 16),), (1, 2, 16, 2.0)),
        "out_weight": scatter_about(key_of[4], (D, D), D ** -0.5, 0.21875),
        "offsets": jax.random.permutation(key_of[5], DILATION_RATE).astype(jnp.int32),
    }


def attend(query_blk, key_blk, value_blk, grad_blk):
    score_scale = query_blk.shape[1] ** -0.5
    scores = jnp.dot(query_blk, key_blk.T, preferred_element_type=jnp.float32) * score_scale
    top_score = jnp.max(scores, axis=1, keepdims=True)
    expo = jnp.exp(scores - top_score)
    probs = expo / jnp.sum(expo, axis=1, keepdims=True)
    probs_low = probs.astype(jnp.bfloat16)
    attn_out = lax.optimization_barrier(jnp.dot(probs_low, value_blk, preferred_element_type=jnp.float32).astype(jnp.bfloat16))
    dprobs = jnp.dot(grad_blk, value_blk.T, preferred_element_type=jnp.float32)
    delta = jnp.sum(grad_blk.astype(jnp.float32) * attn_out.astype(jnp.float32), axis=1, keepdims=True)
    dscores = (probs * (dprobs - delta)).astype(jnp.bfloat16)
    grad_query = (jnp.dot(dscores, key_blk, preferred_element_type=jnp.float32) * score_scale).astype(jnp.bfloat16)
    grad_key = (jnp.dot(dscores.T, query_blk, preferred_element_type=jnp.float32) * score_scale).astype(jnp.bfloat16)
    grad_value = jnp.dot(probs_low.T, grad_blk, preferred_element_type=jnp.float32).astype(jnp.bfloat16)
    return grad_query, grad_key, grad_value, attn_out


def reference(queries, key_rows, value_rows, projected_output_gradient, out_weight, offsets):
    rounds, row_total_count, feature_width = queries.shape
    heads = HEADS
    head_dim = feature_width // heads
    segments = N_TOK // 16
    seg_rows = row_total_count // segments
    weight_split = out_weight.reshape(feature_width, heads, head_dim).astype(jnp.float32)

    def split_heads(array):
        return array.reshape(segments, seg_rows, heads, head_dim).transpose(0, 2, 1, 3).reshape(segments * heads, seg_rows, head_dim)

    def join_heads(array):
        return array.reshape(segments, heads, seg_rows, head_dim).transpose(0, 2, 1, 3).reshape(row_total_count, feature_width)

    grad_q_list = []
    grad_k_list = []
    grad_v_list = []
    weight_total = jnp.zeros((feature_width, feature_width), jnp.float32)
    for round_position in range(rounds):
        phase_shifted = projected_output_gradient[round_position].reshape(row_total_count, DILATION_RATE, feature_width)
        chosen = phase_shifted[:, offsets.astype(jnp.int32), :]
        grad_heads = jnp.einsum('ihj,jhe->ihe', chosen.astype(jnp.float32), weight_split)
        grad_heads = lax.optimization_barrier(grad_heads.astype(jnp.bfloat16)).reshape(row_total_count, feature_width)
        items = (split_heads(queries[round_position]), split_heads(key_rows[round_position]), split_heads(value_rows[round_position]), split_heads(grad_heads))
        grad_query, grad_key, grad_value, attn_out = lax.map(lambda item: attend(*item), items)
        grad_q_list.append(join_heads(grad_query))
        grad_k_list.append(join_heads(grad_key))
        grad_v_list.append(join_heads(grad_value))
        attn_rows = join_heads(attn_out).reshape(row_total_count, heads, head_dim)
        term = jnp.einsum('ihj,ihe->jhe', chosen.astype(jnp.float32), attn_rows.astype(jnp.float32))
        weight_total = weight_total + term.reshape(feature_width, feature_width)
    return jnp.stack(grad_q_list), jnp.stack(grad_k_list), jnp.stack(grad_v_list), weight_total
```

```python
import functools

import jax
import jax.numpy as jnp
from jax import lax
from jax.experimental import pallas as pl
from jax.experimental.pallas import tpu as pltpu
from jax.sharding import PartitionSpec as P

MESH = pl.DeviceIdType.MESH
F32 = jnp.float32
BF16 = jnp.bfloat16
LOG2E = 1.4426950408889634
LANES = 128
PACK = 16


def dot(a, b, ca, cb):
    return lax.dot_general(a, b, (((ca,), (cb,)), ((), ())), preferred_element_type=F32)


def flip_bits(index, mask):
    out = index
    bit = 1
    while bit <= mask:
        if mask & bit:
            out = out + bit - 2 * bit * ((index // bit) % 2)
        bit *= 2
    return out


def main_kernel(
    dims,
    off_ref, q_hbm, k_hbm, v_hbm, w_hbm, x_hbm,
    dq_hbm, dk_hbm, dv_hbm, gw_hbm,
    x, qkv, w, wt, perm, out_t, recv, res, ret, kk, vv, vt1, acc, term, part, half, landed, cross_out, cross_in,
    laid, gw,
    x_sem, in_sem, w_sem, qkv_send, qkv_recv, g_send, g_recv, res_send, ret_recv, attn_send, attn_recv,
    red_send, red_recv, cross_send, cross_recv, out_sem, gw_sem,
):
    rounds, rows, width, heads, head_dim, tok, phases = dims
    seg = heads * rows
    me = lax.axis_index("tok")
    lane = me % heads
    base = me - lane
    order = sorted(range(1, heads), key=lambda s: (-(s // (heads // 2)), -s))
    scale = head_dim ** (-0.5)
    group = heads // 2
    groups = tok // group
    lo = me % group
    hi = me // group
    own = width // tok
    chunks = rows // PACK

    greet = sorted(set(range(1, heads)) | set(group * s for s in range(1, groups)))
    barrier = pltpu.get_barrier_semaphore()
    for s in greet:
        pl.semaphore_signal(barrier, inc=1, device_id={"tok": flip_bits(me, s)}, device_id_type=MESH)

    def load_qkv(r):
        return [
            pltpu.make_async_copy(ref.at[r], qkv.at[r, a], in_sem.at[r, a])
            for a, ref in enumerate((q_hbm, k_hbm, v_hbm))
        ]

    def load_x(r):
        return pltpu.make_async_copy(x_hbm.at[r], x.at[r], x_sem.at[r])

    load_w = pltpu.make_async_copy(w_hbm, w, w_sem)
    for r in range(rounds):
        for copy in load_qkv(r):
            copy.start()
        if r == 0:
            load_w.start()
        load_x(r).start()

    def columns(d):
        return pl.ds(pl.multiple_of(d * rows, rows), rows)

    def send_out(r, first, count, send_sem, recv_sem):
        for s in order:
            d = flip_bits(lane, s)
            pltpu.make_async_remote_copy(
                src_ref=out_t.at[r, pl.ds(first, count), d],
                dst_ref=recv.at[r, pl.ds(first, count), :, columns(lane)],
                send_sem=send_sem.at[r],
                recv_sem=recv_sem.at[r],
                device_id={"tok": base + d},
                device_id_type=MESH,
            ).start()
        pltpu.make_async_copy(
            out_t.at[r, pl.ds(first, count), lane],
            recv.at[r, pl.ds(first, count), :, columns(lane)],
            recv_sem.at[r],
        ).start()

    def turn(r):
        for a, copy in enumerate(load_qkv(r)):
            copy.wait()
            out_t[r, a] = qkv[r, a].T.reshape(heads, head_dim, rows)

    def project(r):
        load_x(r).wait()

        def chunk(c, inner):
            x[r, c] = dot(perm[...], x[r, c], 1, 0).astype(BF16)
            return inner

        lax.fori_loop(0, chunks, chunk, 0)
        for h in range(heads):
            chosen = x[r, :, h * PACK : (h + 1) * PACK, :].reshape(rows, width)
            out_t[r, 3, h] = dot(wt[h * head_dim : (h + 1) * head_dim, :], chosen, 1, 1).astype(BF16)

    turn(0)
    at = lax.broadcasted_iota(jnp.int32, (PACK, PACK * phases), 1)
    at = at - phases * lax.broadcasted_iota(jnp.int32, (PACK, PACK * phases), 0)
    for h in range(heads):
        perm[h * PACK : (h + 1) * PACK, :] = jnp.where(at == off_ref[h], 1.0, 0.0).astype(BF16)
    pl.semaphore_wait(barrier, len(greet))
    send_out(0, 0, 3, qkv_send, qkv_recv)
    load_w.wait()
    wt[...] = w[...].T

    def prepare(r, carry):
        project(r)
        send_out(r, 3, 1, g_send, g_recv)

        @pl.when(r + 1 < rounds)
        def _():
            turn(r + 1)
            send_out(r + 1, 0, 3, qkv_send, qkv_recv)

        return carry

    lax.fori_loop(0, rounds, prepare, 0)

    def send_back(r, a, send_sem, recv_sem):
        for s in order:
            d = flip_bits(lane, s)
            pltpu.make_async_remote_copy(
                src_ref=res.at[r, a, :, columns(d)],
                dst_ref=ret.at[r, a, lane],
                send_sem=send_sem,
                recv_sem=recv_sem,
                device_id={"tok": base + d},
                device_id_type=MESH,
            ).start()
        pltpu.make_async_copy(res.at[r, a, :, columns(lane)], ret.at[r, a, lane], recv_sem).start()

    def send_grads(r):
        for a in range(3):
            send_back(r, a, res_send.at[r, a], ret_recv.at[r, a])

    block = seg // 2
    k_pad = jnp.zeros((LANES - 2 * head_dim, seg), BF16)
    v_pad = jnp.zeros((LANES - head_dim - PACK, seg), BF16)
    ones = jnp.ones((PACK, seg), BF16)

    def attend(r, carry):
        got = recv.at[r, pl.ds(0, 3)]
        pltpu.make_async_copy(got, got, qkv_recv.at[r]).wait()
        kt = recv[r, 1]
        vt = recv[r, 2]
        kk[...] = jnp.concatenate([kt, kt, k_pad], 0).T
        vv[...] = jnp.concatenate([vt, ones, v_pad], 0).T
        vt1[...] = jnp.concatenate([vt, ones], 0)
        acc[...] = jnp.zeros_like(acc)
        pltpu.make_async_copy(recv.at[r, 3], recv.at[r, 3], g_recv.at[r]).wait()

        def q_block(b, inner):
            cols = pl.ds(pl.multiple_of(b * block, block), block)
            qt = recv[r, 0, :, cols].astype(F32)
            gt = recv[r, 3, :, cols]
            gf = gt.astype(F32)
            qc = qt * (scale * LOG2E)
            q_high = qc.astype(BF16)
            q_low = (qc - q_high.astype(F32)).astype(BF16)
            q_two = jnp.concatenate([q_high, q_low, jnp.zeros((LANES - 2 * head_dim, block), BF16)], 0)
            s = dot(kk[...], q_two, 1, 0)
            e = jnp.exp2(s - jnp.max(s, axis=0, keepdims=True)).astype(BF16)
            both = dot(vt1[...], e, 1, 0)
            inv = 1.0 / both[head_dim : head_dim + 1]
            ot = (both[:head_dim] * inv).astype(BF16)
            res[r, 3, :, cols] = ot
            minus = -jnp.sum(gf * ot.astype(F32), axis=0, keepdims=True)
            m_high = minus.astype(BF16).astype(F32)
            row = lax.broadcasted_iota(jnp.int32, (PACK, block), 0)
            m_two = jnp.where(row == 0, m_high, jnp.where(row == 1, minus - m_high, 0.0)).astype(BF16)
            g_two = jnp.concatenate([gt, m_two, jnp.zeros((LANES - head_dim - PACK, block), BF16)], 0)
            ds = e * dot(vv[...], g_two, 1, 0).astype(BF16)
            res[r, 0, :, cols] = (dot(kt, ds, 1, 0) * (inv * scale)).astype(BF16)
            qs = (qt * (inv * scale)).astype(BF16)
            gs = (gf * inv).astype(BF16)
            zero = jnp.zeros((head_dim, block), BF16)
            right = jnp.concatenate(
                [
                    jnp.concatenate([gs, zero], 1),
                    jnp.concatenate([zero, qs], 1),
                    jnp.zeros((LANES - 2 * head_dim, 2 * block), BF16),
                ],
                0,
            )
            acc[...] += dot(jnp.concatenate([e, ds], 1), right, 1, 1)
            return inner

        lax.fori_loop(0, seg // block, q_block, 0)
        send_back(r, 3, attn_send.at[r], attn_recv.at[r])
        t = acc[...].astype(BF16).T
        res[r, 2] = t[:head_dim]
        res[r, 1] = t[head_dim : 2 * head_dim]

        @pl.when(r == 1)
        def _():
            send_grads(0)

        return carry

    lax.fori_loop(0, rounds, attend, 0)
    send_grads(1)

    term[...] = jnp.zeros_like(term)

    def finish(r, carry):
        pltpu.make_async_copy(ret.at[r, 3], ret.at[r, 3], attn_recv.at[r]).wait()
        for h in range(heads):
            chosen = x[r, :, h * PACK : (h + 1) * PACK, :].reshape(rows, width)
            here = pl.ds(h * head_dim, head_dim)
            term[here, :] += dot(ret[r, 3, h], chosen, 1, 0)
        return carry

    lax.fori_loop(0, rounds, finish, 0)
    part[...] = term[...].T.reshape(groups, group, own, width)
    half[...] = part[...].astype(BF16)

    def near(s):
        return pltpu.make_async_remote_copy(
            src_ref=half.at[:, flip_bits(lo, s)],
            dst_ref=landed.at[lo],
            send_sem=red_send.at[s],
            recv_sem=red_recv.at[s],
            device_id={"tok": hi * group + flip_bits(lo, s)},
            device_id_type=MESH,
        )

    def far(s):
        return pltpu.make_async_remote_copy(
            src_ref=cross_out.at[flip_bits(hi, s)],
            dst_ref=cross_in.at[hi],
            send_sem=cross_send.at[s],
            recv_sem=cross_recv.at[s],
            device_id={"tok": flip_bits(hi, s) * group + lo},
            device_id_type=MESH,
        )

    def lay_out(r):
        for a, ref in enumerate((dq_hbm, dk_hbm, dv_hbm)):
            pltpu.make_async_copy(ret.at[r, a], ret.at[r, a], ret_recv.at[r, a]).wait()
            laid[r, a] = ret[r, a].reshape(width, rows).T
            pltpu.make_async_copy(laid.at[r, a], ref.at[r], out_sem.at[r, a]).start()

    for s in range(1, group):
        near(s).start()
    for r in range(2, rounds - 1):
        send_grads(r)
    lay_out(0)
    for s in range(1, group):
        near(s).wait()
    for j in range(groups):
        total = part[j, lo]
        for s in range(1, group):
            total = total + landed[flip_bits(lo, s), j].astype(F32)
        part[j, lo] = total
        cross_out[j] = total.astype(BF16)
    for s in range(1, groups):
        far(s).start()
    send_grads(rounds - 1)
    for r in range(1, rounds - 1):
        lay_out(r)
    for s in range(1, groups):
        far(s).wait()
    total = part[hi, lo]
    for s in range(1, groups):
        total = total + cross_in[flip_bits(hi, s)].astype(F32)
    gw[...] = total
    pltpu.make_async_copy(gw, gw_hbm, gw_sem).start()
    lay_out(rounds - 1)

    for r in range(rounds):
        blocks = pl.ds(0, heads - 1)
        sent = out_t.at[r, pl.ds(0, 3), blocks]
        pltpu.make_async_copy(sent, sent, qkv_send.at[r]).wait()
        sent = out_t.at[r, 3, blocks]
        pltpu.make_async_copy(sent, sent, g_send.at[r]).wait()
        for a in range(3):
            sent = ret.at[r, a, blocks]
            pltpu.make_async_copy(sent, sent, res_send.at[r, a]).wait()
        sent = ret.at[r, 3, blocks]
        pltpu.make_async_copy(sent, sent, attn_send.at[r]).wait()
    for r in range(rounds):
        for a, ref in enumerate((dq_hbm, dk_hbm, dv_hbm)):
            pltpu.make_async_copy(laid.at[r, a], ref.at[r], out_sem.at[r, a]).wait()
    pltpu.make_async_copy(gw, gw_hbm, gw_sem).wait()


def hand_over(*refs):
    count = (len(refs) - 2) // 3
    got, given, kept = refs[:count], refs[count : 2 * count], refs[2 * count : 3 * count]
    in_sem, out_sem = refs[3 * count :]
    into = [pltpu.make_async_copy(got[i], kept[i], in_sem.at[i]) for i in range(count)]
    out_of = [pltpu.make_async_copy(kept[i], given[i], out_sem.at[i]) for i in range(count)]
    for copy in into:
        copy.start()
    for i in range(count):
        into[i].wait()
        out_of[i].start()
    for copy in out_of:
        copy.wait()


def local(queries, key_rows, value_rows, projected_output_gradient, out_weight, offsets):
    rounds, rows, width = queries.shape
    heads = offsets.shape[0]
    head_dim = width // heads
    tok = lax.axis_size("tok")
    phases = projected_output_gradient.shape[1] // rows
    seg = heads * rows
    own = width // tok
    group = heads // 2
    groups = tok // group
    dims = (rounds, rows, width, heads, head_dim, tok, phases)
    tokens = projected_output_gradient.reshape(rounds, rows // PACK, PACK * phases, width)
    hbm = pl.BlockSpec(memory_space=pl.ANY)
    rows_shape = jax.ShapeDtypeStruct((rounds, rows, width), BF16)
    out_shape = (rows_shape, rows_shape, rows_shape, jax.ShapeDtypeStruct((own, width), F32))
    dma = pltpu.SemaphoreType.DMA
    results = pl.pallas_call(
        functools.partial(main_kernel, dims),
        out_shape=out_shape,
        in_specs=[pl.BlockSpec(memory_space=pltpu.SMEM)] + [hbm] * 5,
        out_specs=(hbm,) * 4,
        scratch_shapes=[
            pltpu.VMEM((rounds, rows // PACK, PACK * phases, width), BF16),
            pltpu.VMEM((rounds, 3, rows, width), BF16),
            pltpu.VMEM((width, width), BF16),
            pltpu.VMEM((width, width), BF16),
            pltpu.VMEM((PACK * heads, PACK * phases), BF16),
            pltpu.VMEM((rounds, 4, heads, head_dim, rows), BF16),
            pltpu.VMEM((rounds, 4, head_dim, seg), BF16),
            pltpu.VMEM((rounds, 4, head_dim, seg), BF16),
            pltpu.VMEM((rounds, 4, heads, head_dim, rows), BF16),
            pltpu.VMEM((seg, LANES), BF16),
            pltpu.VMEM((seg, LANES), BF16),
            pltpu.VMEM((head_dim + PACK, seg), BF16),
            pltpu.VMEM((seg, LANES), F32),
            pltpu.VMEM((width, width), F32),
            pltpu.VMEM((groups, group, own, width), F32),
            pltpu.VMEM((groups, group, own, width), BF16),
            pltpu.VMEM((group, groups, own, width), BF16),
            pltpu.VMEM((groups, own, width), BF16),
            pltpu.VMEM((groups, own, width), BF16),
            pltpu.VMEM((rounds, 3, rows, width), BF16),
            pltpu.VMEM((own, width), F32),
            dma((rounds,)),
            dma((rounds, 3)),
            dma,
            dma((rounds,)),
            dma((rounds,)),
            dma((rounds,)),
            dma((rounds,)),
            dma((rounds, 3)),
            dma((rounds, 3)),
            dma((rounds,)),
            dma((rounds,)),
            dma((group,)),
            dma((group,)),
            dma((groups,)),
            dma((groups,)),
            dma((rounds, 3)),
            dma,
        ],
        compiler_params=pltpu.CompilerParams(
            collective_id=0, has_side_effects=True, vmem_limit_bytes=66000000
        ),
        name="branch_backward",
    )(offsets, queries, key_rows, value_rows, out_weight, tokens)
    return pl.pallas_call(
        hand_over,
        out_shape=out_shape,
        in_specs=[hbm] * 4,
        out_specs=(hbm,) * 4,
        scratch_shapes=[pltpu.VMEM(a.shape, a.dtype) for a in out_shape] + [dma((4,)), dma((4,))],
        name="hand_over",
    )(*results)


def solution(mesh):
    placed = (
        P("slides", "tok", None),
        P("slides", "tok", None),
        P("slides", "tok", None),
        P("slides", "tok", None),
        P(),
        P(),
    )
    return jax.shard_map(
        local,
        mesh=mesh,
        in_specs=placed,
        out_specs=(
            P("slides", "tok", None),
            P("slides", "tok", None),
            P("slides", "tok", None),
            P(("slides", "tok"), None),
        ),
        check_vma=False,
    )
```

```python
import functools

import jax
import jax.numpy as jnp
from jax import lax
from jax.experimental import pallas as pl
from jax.experimental.pallas import tpu as pltpu
from jax.sharding import PartitionSpec as P

MESH = pl.DeviceIdType.MESH
F32 = jnp.float32
BF16 = jnp.bfloat16
LOG2E = 1.4426950408889634
LANES = 128
PACK = 16


def dot(a, b, ca, cb):
    return lax.dot_general(a, b, (((ca,), (cb,)), ((), ())), preferred_element_type=F32)


def flip_bits(index, mask):
    out = index
    bit = 1
    while bit <= mask:
        if mask & bit:
            out = out + bit - 2 * bit * ((index // bit) % 2)
        bit *= 2
    return out


def main_kernel(
    dims,
    off_ref, q_hbm, k_hbm, v_hbm, w_hbm, x_hbm,
    dq_hbm, dk_hbm, dv_hbm, gw_hbm,
    x, qkv, w, wt, perm, out_t, recv, res, ret, kk, vv, vt1, acc, term, part, half, landed, cross_out, cross_in,
    laid, gw,
    x_sem, in_sem, w_sem, qkv_send, qkv_recv, g_send, g_recv, res_send, ret_recv, attn_send, attn_recv,
    red_send, red_recv, cross_send, cross_recv, out_sem, gw_sem,
):
    rounds, rows, width, heads, head_dim, tok, phases = dims
    seg = heads * rows
    me = lax.axis_index("tok")
    lane = me % heads
    base = me - lane
    order = sorted(range(1, heads), key=lambda s: (-(s // (heads // 2)), -s))
    across = [s for s in order if s >= heads // 2]
    within = [s for s in order if s < heads // 2]
    quarter = lane // (heads // 4)
    outer = jnp.logical_or(quarter == 0, quarter == 3)
    inner = jnp.logical_not(outer)
    scale = head_dim ** (-0.5)
    group = heads // 2
    groups = tok // group
    lo = me % group
    hi = me // group
    own = width // tok
    chunks = rows // PACK

    greet = sorted(set(range(1, heads)) | set(group * s for s in range(1, groups)))
    barrier = pltpu.get_barrier_semaphore()
    for s in greet:
        pl.semaphore_signal(barrier, inc=1, device_id={"tok": flip_bits(me, s)}, device_id_type=MESH)

    def load_qkv(r):
        return [
            pltpu.make_async_copy(ref.at[r], qkv.at[r, a], in_sem.at[r, a])
            for a, ref in enumerate((q_hbm, k_hbm, v_hbm))
        ]

    def load_x(r):
        return pltpu.make_async_copy(x_hbm.at[r], x.at[r], x_sem.at[r])

    load_w = pltpu.make_async_copy(w_hbm, w, w_sem)
    for r in range(rounds):
        for copy in load_qkv(r):
            copy.start()
        if r == 0:
            load_w.start()
        load_x(r).start()

    def columns(d):
        return pl.ds(pl.multiple_of(d * rows, rows), rows)

    def send_to(peers, r, first, count, send_sem, recv_sem):
        for s in peers:
            d = flip_bits(lane, s)
            pltpu.make_async_remote_copy(
                src_ref=out_t.at[r, pl.ds(first, count), d],
                dst_ref=recv.at[r, pl.ds(first, count), :, columns(lane)],
                send_sem=send_sem.at[r],
                recv_sem=recv_sem.at[r],
                device_id={"tok": base + d},
                device_id_type=MESH,
            ).start()

    def send_across(r, first, count, send_sem, recv_sem):
        send_to(across, r, first, count, send_sem, recv_sem)

    def send_within(r, first, count, send_sem, recv_sem):
        send_to(within, r, first, count, send_sem, recv_sem)
        pltpu.make_async_copy(
            out_t.at[r, pl.ds(first, count), lane],
            recv.at[r, pl.ds(first, count), :, columns(lane)],
            recv_sem.at[r],
        ).start()

    def turn(r):
        for a, copy in enumerate(load_qkv(r)):
            copy.wait()
            out_t[r, a] = qkv[r, a].T.reshape(heads, head_dim, rows)

    def project(r):
        load_x(r).wait()

        def chunk(c, inner):
            x[r, c] = dot(perm[...], x[r, c], 1, 0).astype(BF16)
            return inner

        lax.fori_loop(0, chunks, chunk, 0)
        for h in range(heads):
            chosen = x[r, :, h * PACK : (h + 1) * PACK, :].reshape(rows, width)
            out_t[r, 3, h] = dot(wt[h * head_dim : (h + 1) * head_dim, :], chosen, 1, 1).astype(BF16)

    turn(0)
    at = lax.broadcasted_iota(jnp.int32, (PACK, PACK * phases), 1)
    at = at - phases * lax.broadcasted_iota(jnp.int32, (PACK, PACK * phases), 0)
    for h in range(heads):
        perm[h * PACK : (h + 1) * PACK, :] = jnp.where(at == off_ref[h], 1.0, 0.0).astype(BF16)
    pl.semaphore_wait(barrier, len(greet))

    @pl.when(outer)
    def _():
        send_across(0, 0, 3, qkv_send, qkv_recv)

    send_within(0, 0, 3, qkv_send, qkv_recv)

    @pl.when(inner)
    def _():
        send_across(0, 0, 3, qkv_send, qkv_recv)

    load_w.wait()
    wt[...] = w[...].T

    def prepare(r, carry):
        project(r)

        @pl.when(jnp.logical_and(r == 0, outer))
        def _():
            send_across(r, 3, 1, g_send, g_recv)

        send_within(r, 3, 1, g_send, g_recv)

        @pl.when(inner)
        def _():
            send_across(r, 3, 1, g_send, g_recv)

        @pl.when(r + 1 < rounds)
        def _():
            turn(r + 1)
            send_within(r + 1, 0, 3, qkv_send, qkv_recv)

            @pl.when(inner)
            def _():
                send_across(r + 1, 0, 3, qkv_send, qkv_recv)

        return carry

    lax.fori_loop(0, rounds, prepare, 0)

    def send_back(r, a, send_sem, recv_sem):
        def send_to_all(peers):
            for s in peers:
                d = flip_bits(lane, s)
                pltpu.make_async_remote_copy(
                    src_ref=res.at[r, a, :, columns(d)],
                    dst_ref=ret.at[r, a, lane],
                    send_sem=send_sem,
                    recv_sem=recv_sem,
                    device_id={"tok": base + d},
                    device_id_type=MESH,
                ).start()

        @pl.when(outer)
        def _():
            send_to_all(across)

        send_to_all(within)
        pltpu.make_async_copy(res.at[r, a, :, columns(lane)], ret.at[r, a, lane], recv_sem).start()

        @pl.when(inner)
        def _():
            send_to_all(across)

    def send_attn(r):
        send_back(r, 3, attn_send.at[r], attn_recv.at[r])

    def send_grad(r, a):
        send_back(r, a, res_send.at[r, a], ret_recv.at[r, a])

    block = seg // 2
    k_pad = jnp.zeros((LANES - 2 * head_dim, seg), BF16)
    v_pad = jnp.zeros((LANES - head_dim - PACK, seg), BF16)
    ones = jnp.ones((PACK, seg), BF16)

    def attend(r, carry):
        got = recv.at[r, pl.ds(0, 3)]
        pltpu.make_async_copy(got, got, qkv_recv.at[r]).wait()
        pltpu.make_async_copy(recv.at[r, 3], recv.at[r, 3], g_recv.at[r]).wait()

        @pl.when(jnp.logical_and(outer, r + 1 < rounds))
        def _():
            send_across(r + 1, 0, 3, qkv_send, qkv_recv)
            send_across(r + 1, 3, 1, g_send, g_recv)

        @pl.when(r == rounds - 2)
        def _():
            def one(i, inner_carry):
                send_attn(i)
                return inner_carry

            lax.fori_loop(0, rounds - 2, one, 0)
            send_grad(0, 0)
            send_grad(0, 1)

        kt = recv[r, 1]
        vt = recv[r, 2]
        kk[...] = jnp.concatenate([kt, kt, k_pad], 0).T
        vv[...] = jnp.concatenate([vt, ones, v_pad], 0).T
        vt1[...] = jnp.concatenate([vt, ones], 0)
        acc[...] = jnp.zeros_like(acc)
        def q_block(b, inner):
            cols = pl.ds(pl.multiple_of(b * block, block), block)
            qt = recv[r, 0, :, cols].astype(F32)
            gt = recv[r, 3, :, cols]
            gf = gt.astype(F32)
            qc = qt * (scale * LOG2E)
            q_high = qc.astype(BF16)
            q_low = (qc - q_high.astype(F32)).astype(BF16)
            q_two = jnp.concatenate([q_high, q_low, jnp.zeros((LANES - 2 * head_dim, block), BF16)], 0)
            s = dot(kk[...], q_two, 1, 0)
            e = jnp.exp2(s - jnp.max(s, axis=0, keepdims=True)).astype(BF16)
            both = dot(vt1[...], e, 1, 0)
            inv = 1.0 / both[head_dim : head_dim + 1]
            ot = (both[:head_dim] * inv).astype(BF16)
            res[r, 3, :, cols] = ot
            minus = -jnp.sum(gf * ot.astype(F32), axis=0, keepdims=True)
            m_high = minus.astype(BF16).astype(F32)
            row = lax.broadcasted_iota(jnp.int32, (PACK, block), 0)
            m_two = jnp.where(row == 0, m_high, jnp.where(row == 1, minus - m_high, 0.0)).astype(BF16)
            g_two = jnp.concatenate([gt, m_two, jnp.zeros((LANES - head_dim - PACK, block), BF16)], 0)
            ds = e * dot(vv[...], g_two, 1, 0).astype(BF16)
            res[r, 0, :, cols] = (dot(kt, ds, 1, 0) * (inv * scale)).astype(BF16)
            qs = (qt * (inv * scale)).astype(BF16)
            gs = (gf * inv).astype(BF16)
            zero = jnp.zeros((head_dim, block), BF16)
            right = jnp.concatenate(
                [
                    jnp.concatenate([gs, zero], 1),
                    jnp.concatenate([zero, qs], 1),
                    jnp.zeros((LANES - 2 * head_dim, 2 * block), BF16),
                ],
                0,
            )
            acc[...] += dot(jnp.concatenate([e, ds], 1), right, 1, 1)
            return inner

        lax.fori_loop(0, seg // block, q_block, 0)

        @pl.when(r >= rounds - 2)
        def _():
            send_attn(r)

        t = acc[...].astype(BF16).T
        res[r, 2] = t[:head_dim]
        res[r, 1] = t[head_dim : 2 * head_dim]

        @pl.when(r == rounds - 2)
        def _():
            send_grad(0, 2)

        return carry

    lax.fori_loop(0, rounds, attend, 0)
    later = [(r, a) for r in range(rounds) for a in range(3)][3:]
    for piece in later[:3]:
        send_grad(*piece)

    term[...] = jnp.zeros_like(term)

    def finish(r, carry):
        pltpu.make_async_copy(ret.at[r, 3], ret.at[r, 3], attn_recv.at[r]).wait()
        for h in range(heads):
            chosen = x[r, :, h * PACK : (h + 1) * PACK, :].reshape(rows, width)
            here = pl.ds(h * head_dim, head_dim)
            term[here, :] += dot(ret[r, 3, h], chosen, 1, 0)
        return carry

    lax.fori_loop(0, rounds, finish, 0)
    part[...] = term[...].T.reshape(groups, group, own, width)
    half[...] = part[...].astype(BF16)

    def near(s):
        return pltpu.make_async_remote_copy(
            src_ref=half.at[:, flip_bits(lo, s)],
            dst_ref=landed.at[lo],
            send_sem=red_send.at[s],
            recv_sem=red_recv.at[s],
            device_id={"tok": hi * group + flip_bits(lo, s)},
            device_id_type=MESH,
        )

    def far(s):
        return pltpu.make_async_remote_copy(
            src_ref=cross_out.at[flip_bits(hi, s)],
            dst_ref=cross_in.at[hi],
            send_sem=cross_send.at[s],
            recv_sem=cross_recv.at[s],
            device_id={"tok": flip_bits(hi, s) * group + lo},
            device_id_type=MESH,
        )

    def lay_out(r):
        for a, ref in enumerate((dq_hbm, dk_hbm, dv_hbm)):
            pltpu.make_async_copy(ret.at[r, a], ret.at[r, a], ret_recv.at[r, a]).wait()
            laid[r, a] = ret[r, a].reshape(width, rows).T
            pltpu.make_async_copy(laid.at[r, a], ref.at[r], out_sem.at[r, a]).start()

    beside = later[3:8]
    for s in range(1, group):
        near(s).start()
        for piece in beside[(s - 1) * len(beside) // (group - 1) : s * len(beside) // (group - 1)]:
            send_grad(*piece)
    for piece in later[8:9]:
        send_grad(*piece)
    lay_out(0)
    for s in range(1, group):
        near(s).wait()
    for j in range(groups):
        total = part[j, lo]
        for s in range(1, group):
            total = total + landed[flip_bits(lo, s), j].astype(F32)
        part[j, lo] = total
        cross_out[j] = total.astype(BF16)
    for s in range(1, groups):
        far(s).start()
    for piece in later[9:]:
        send_grad(*piece)
    for r in range(1, rounds - 1):
        lay_out(r)
    for s in range(1, groups):
        far(s).wait()
    total = part[hi, lo]
    for s in range(1, groups):
        total = total + cross_in[flip_bits(hi, s)].astype(F32)
    gw[...] = total
    pltpu.make_async_copy(gw, gw_hbm, gw_sem).start()
    lay_out(rounds - 1)

    for r in range(rounds):
        blocks = pl.ds(0, heads - 1)
        sent = out_t.at[r, pl.ds(0, 3), blocks]
        pltpu.make_async_copy(sent, sent, qkv_send.at[r]).wait()
        sent = out_t.at[r, 3, blocks]
        pltpu.make_async_copy(sent, sent, g_send.at[r]).wait()
        for a in range(3):
            sent = ret.at[r, a, blocks]
            pltpu.make_async_copy(sent, sent, res_send.at[r, a]).wait()
        sent = ret.at[r, 3, blocks]
        pltpu.make_async_copy(sent, sent, attn_send.at[r]).wait()
    for r in range(rounds):
        for a, ref in enumerate((dq_hbm, dk_hbm, dv_hbm)):
            pltpu.make_async_copy(laid.at[r, a], ref.at[r], out_sem.at[r, a]).wait()
    pltpu.make_async_copy(gw, gw_hbm, gw_sem).wait()


def hand_over(*refs):
    count = (len(refs) - 2) // 3
    got, given, kept = refs[:count], refs[count : 2 * count], refs[2 * count : 3 * count]
    in_sem, out_sem = refs[3 * count :]
    into = [pltpu.make_async_copy(got[i], kept[i], in_sem.at[i]) for i in range(count)]
    out_of = [pltpu.make_async_copy(kept[i], given[i], out_sem.at[i]) for i in range(count)]
    for copy in into:
        copy.start()
    for i in range(count):
        into[i].wait()
        out_of[i].start()
    for copy in out_of:
        copy.wait()


def local(queries, key_rows, value_rows, projected_output_gradient, out_weight, offsets):
    rounds, rows, width = queries.shape
    heads = offsets.shape[0]
    head_dim = width // heads
    tok = lax.axis_size("tok")
    phases = projected_output_gradient.shape[1] // rows
    seg = heads * rows
    own = width // tok
    group = heads // 2
    groups = tok // group
    dims = (rounds, rows, width, heads, head_dim, tok, phases)
    tokens = projected_output_gradient.reshape(rounds, rows // PACK, PACK * phases, width)
    hbm = pl.BlockSpec(memory_space=pl.ANY)
    rows_shape = jax.ShapeDtypeStruct((rounds, rows, width), BF16)
    out_shape = (rows_shape, rows_shape, rows_shape, jax.ShapeDtypeStruct((own, width), F32))
    dma = pltpu.SemaphoreType.DMA
    results = pl.pallas_call(
        functools.partial(main_kernel, dims),
        out_shape=out_shape,
        in_specs=[pl.BlockSpec(memory_space=pltpu.SMEM)] + [hbm] * 5,
        out_specs=(hbm,) * 4,
        scratch_shapes=[
            pltpu.VMEM((rounds, rows // PACK, PACK * phases, width), BF16),
            pltpu.VMEM((rounds, 3, rows, width), BF16),
            pltpu.VMEM((width, width), BF16),
            pltpu.VMEM((width, width), BF16),
            pltpu.VMEM((PACK * heads, PACK * phases), BF16),
            pltpu.VMEM((rounds, 4, heads, head_dim, rows), BF16),
            pltpu.VMEM((rounds, 4, head_dim, seg), BF16),
            pltpu.VMEM((rounds, 4, head_dim, seg), BF16),
            pltpu.VMEM((rounds, 4, heads, head_dim, rows), BF16),
            pltpu.VMEM((seg, LANES), BF16),
            pltpu.VMEM((seg, LANES), BF16),
            pltpu.VMEM((head_dim + PACK, seg), BF16),
            pltpu.VMEM((seg, LANES), F32),
            pltpu.VMEM((width, width), F32),
            pltpu.VMEM((groups, group, own, width), F32),
            pltpu.VMEM((groups, group, own, width), BF16),
            pltpu.VMEM((group, groups, own, width), BF16),
            pltpu.VMEM((groups, own, width), BF16),
            pltpu.VMEM((groups, own, width), BF16),
            pltpu.VMEM((rounds, 3, rows, width), BF16),
            pltpu.VMEM((own, width), F32),
            dma((rounds,)),
            dma((rounds, 3)),
            dma,
            dma((rounds,)),
            dma((rounds,)),
            dma((rounds,)),
            dma((rounds,)),
            dma((rounds, 3)),
            dma((rounds, 3)),
            dma((rounds,)),
            dma((rounds,)),
            dma((group,)),
            dma((group,)),
            dma((groups,)),
            dma((groups,)),
            dma((rounds, 3)),
            dma,
        ],
        compiler_params=pltpu.CompilerParams(
            collective_id=0, has_side_effects=True, vmem_limit_bytes=66000000
        ),
        name="branch_backward",
    )(offsets, queries, key_rows, value_rows, out_weight, tokens)
    return pl.pallas_call(
        hand_over,
        out_shape=out_shape,
        in_specs=[hbm] * 4,
        out_specs=(hbm,) * 4,
        scratch_shapes=[pltpu.VMEM(a.shape, a.dtype) for a in out_shape] + [dma((4,)), dma((4,))],
        name="hand_over",
    )(*results)


def solution(mesh):
    placed = (
        P("slides", "tok", None),
        P("slides", "tok", None),
        P("slides", "tok", None),
        P("slides", "tok", None),
        P(),
        P(),
    )
    return jax.shard_map(
        local,
        mesh=mesh,
        in_specs=placed,
        out_specs=(
            P("slides", "tok", None),
            P("slides", "tok", None),
            P("slides", "tok", None),
            P(("slides", "tok"), None),
        ),
        check_vma=False,
    )
```

```python
import functools

import jax
import jax.numpy as jnp
from jax import lax
from jax.experimental import pallas as pl
from jax.experimental.pallas import tpu as pltpu
from jax.sharding import PartitionSpec as P

MESH = pl.DeviceIdType.MESH
F32 = jnp.float32
BF16 = jnp.bfloat16
LOG2E = 1.4426950408889634
LANES = 128
PACK = 16


def dot(a, b, ca, cb):
    return lax.dot_general(a, b, (((ca,), (cb,)), ((), ())), preferred_element_type=F32)


def flip_bits(index, mask):
    out = index
    bit = 1
    while bit <= mask:
        if mask & bit:
            out = out + bit - 2 * bit * ((index // bit) % 2)
        bit *= 2
    return out


def main_kernel(
    dims,
    off_ref, q_hbm, k_hbm, v_hbm, w_hbm, x_hbm,
    dq_hbm, dk_hbm, dv_hbm, gw_hbm,
    x, qkv, w, wt, perm, out_t, recv, res, ret, kk, vv, vt1, acc, term, part, half, pair_in, near_out, landed, cross_out, cross_in, mine,
    laid, gw,
    x_sem, in_sem, w_sem, qkv_send, qkv_recv, g_send, g_recv, res_send, ret_recv, attn_send, attn_recv,
    pair_send, pair_recv, red_send, red_recv, cross_send, cross_recv, out_sem, gw_sem,
):
    rounds, rows, width, heads, head_dim, tok, phases = dims
    seg = heads * rows
    me = lax.axis_index("tok")
    lane = me % heads
    base = me - lane
    order = sorted(range(1, heads), key=lambda s: (-(s // (heads // 2)), -s))
    across = [s for s in order if s >= heads // 2]
    within = [s for s in order if s < heads // 2]
    quarter = lane // (heads // 4)
    outer = jnp.logical_or(quarter == 0, quarter == 3)
    inner = jnp.logical_not(outer)
    scale = head_dim ** (-0.5)
    group = heads // 2
    groups = tok // group
    lo = me % group
    hi = me // group
    chip = lo // 2
    core = lo % 2
    chips = group // 2
    own = width // tok
    chunks = rows // PACK

    greet = sorted(set(range(1, heads)) | set(group * s for s in range(1, groups)))
    barrier = pltpu.get_barrier_semaphore()
    for s in greet:
        pl.semaphore_signal(barrier, inc=1, device_id={"tok": flip_bits(me, s)}, device_id_type=MESH)

    def load_qkv(r):
        return [
            pltpu.make_async_copy(ref.at[r], qkv.at[r, a], in_sem.at[r, a])
            for a, ref in enumerate((q_hbm, k_hbm, v_hbm))
        ]

    def load_x(r):
        return pltpu.make_async_copy(x_hbm.at[r], x.at[r], x_sem.at[r])

    load_w = pltpu.make_async_copy(w_hbm, w, w_sem)
    for r in range(rounds):
        for copy in load_qkv(r):
            copy.start()
        if r == 0:
            load_w.start()
        load_x(r).start()

    def columns(d):
        return pl.ds(pl.multiple_of(d * rows, rows), rows)

    def send_to(peers, r, first, count, send_sem, recv_sem):
        for s in peers:
            d = flip_bits(lane, s)
            pltpu.make_async_remote_copy(
                src_ref=out_t.at[r, pl.ds(first, count), d],
                dst_ref=recv.at[r, pl.ds(first, count), :, columns(lane)],
                send_sem=send_sem.at[r],
                recv_sem=recv_sem.at[r],
                device_id={"tok": base + d},
                device_id_type=MESH,
            ).start()

    def send_across(r, first, count, send_sem, recv_sem):
        send_to(across, r, first, count, send_sem, recv_sem)

    def send_within(r, first, count, send_sem, recv_sem):
        send_to(within, r, first, count, send_sem, recv_sem)
        pltpu.make_async_copy(
            out_t.at[r, pl.ds(first, count), lane],
            recv.at[r, pl.ds(first, count), :, columns(lane)],
            recv_sem.at[r],
        ).start()

    def turn(r):
        for a, copy in enumerate(load_qkv(r)):
            copy.wait()
            out_t[r, a] = qkv[r, a].T.reshape(heads, head_dim, rows)

    def project(r):
        load_x(r).wait()

        def chunk(c, inner):
            x[r, c] = dot(perm[...], x[r, c], 1, 0).astype(BF16)
            return inner

        lax.fori_loop(0, chunks, chunk, 0)
        for h in range(heads):
            chosen = x[r, :, h * PACK : (h + 1) * PACK, :].reshape(rows, width)
            out_t[r, 3, h] = dot(wt[h * head_dim : (h + 1) * head_dim, :], chosen, 1, 1).astype(BF16)

    turn(0)
    at = lax.broadcasted_iota(jnp.int32, (PACK, PACK * phases), 1)
    at = at - phases * lax.broadcasted_iota(jnp.int32, (PACK, PACK * phases), 0)
    for h in range(heads):
        perm[h * PACK : (h + 1) * PACK, :] = jnp.where(at == off_ref[h], 1.0, 0.0).astype(BF16)
    pl.semaphore_wait(barrier, len(greet))

    @pl.when(outer)
    def _():
        send_across(0, 0, 3, qkv_send, qkv_recv)

    send_within(0, 0, 3, qkv_send, qkv_recv)

    @pl.when(inner)
    def _():
        send_across(0, 0, 3, qkv_send, qkv_recv)

    load_w.wait()
    wt[...] = w[...].T

    def prepare(r, carry):
        project(r)

        @pl.when(jnp.logical_and(r == 0, outer))
        def _():
            send_across(r, 3, 1, g_send, g_recv)

        send_within(r, 3, 1, g_send, g_recv)

        @pl.when(inner)
        def _():
            send_across(r, 3, 1, g_send, g_recv)

        @pl.when(r + 1 < rounds)
        def _():
            turn(r + 1)
            send_within(r + 1, 0, 3, qkv_send, qkv_recv)

            @pl.when(inner)
            def _():
                send_across(r + 1, 0, 3, qkv_send, qkv_recv)

        return carry

    lax.fori_loop(0, rounds, prepare, 0)

    def send_back(r, a, send_sem, recv_sem):
        def send_to_all(peers):
            for s in peers:
                d = flip_bits(lane, s)
                pltpu.make_async_remote_copy(
                    src_ref=res.at[r, a, :, columns(d)],
                    dst_ref=ret.at[r, a, lane],
                    send_sem=send_sem,
                    recv_sem=recv_sem,
                    device_id={"tok": base + d},
                    device_id_type=MESH,
                ).start()

        @pl.when(outer)
        def _():
            send_to_all(across)

        send_to_all(within)
        pltpu.make_async_copy(res.at[r, a, :, columns(lane)], ret.at[r, a, lane], recv_sem).start()

        @pl.when(inner)
        def _():
            send_to_all(across)

    def send_attn(r):
        send_back(r, 3, attn_send.at[r], attn_recv.at[r])

    def send_grad(r, a):
        send_back(r, a, res_send.at[r, a], ret_recv.at[r, a])

    block = seg // 2
    k_pad = jnp.zeros((LANES - 2 * head_dim, seg), BF16)
    v_pad = jnp.zeros((LANES - head_dim - PACK, seg), BF16)
    ones = jnp.ones((PACK, seg), BF16)

    def attend(r, carry):
        got = recv.at[r, pl.ds(0, 3)]
        pltpu.make_async_copy(got, got, qkv_recv.at[r]).wait()
        pltpu.make_async_copy(recv.at[r, 3], recv.at[r, 3], g_recv.at[r]).wait()

        @pl.when(jnp.logical_and(outer, r + 1 < rounds))
        def _():
            send_across(r + 1, 0, 3, qkv_send, qkv_recv)
            send_across(r + 1, 3, 1, g_send, g_recv)

        @pl.when(r == rounds - 2)
        def _():
            def one(i, inner_carry):
                send_attn(i)
                return inner_carry

            lax.fori_loop(0, rounds - 2, one, 0)
            send_grad(0, 0)
            send_grad(0, 1)

        kt = recv[r, 1]
        vt = recv[r, 2]
        kk[...] = jnp.concatenate([kt, kt, k_pad], 0).T
        vv[...] = jnp.concatenate([vt, ones, v_pad], 0).T
        vt1[...] = jnp.concatenate([vt, ones], 0)
        acc[...] = jnp.zeros_like(acc)
        def q_block(b, inner):
            cols = pl.ds(pl.multiple_of(b * block, block), block)
            qt = recv[r, 0, :, cols].astype(F32)
            gt = recv[r, 3, :, cols]
            gf = gt.astype(F32)
            qc = qt * (scale * LOG2E)
            q_high = qc.astype(BF16)
            q_low = (qc - q_high.astype(F32)).astype(BF16)
            q_two = jnp.concatenate([q_high, q_low, jnp.zeros((LANES - 2 * head_dim, block), BF16)], 0)
            s = dot(kk[...], q_two, 1, 0)
            e = jnp.exp2(s - jnp.max(s, axis=0, keepdims=True)).astype(BF16)
            both = dot(vt1[...], e, 1, 0)
            inv = 1.0 / both[head_dim : head_dim + 1]
            ot = (both[:head_dim] * inv).astype(BF16)
            res[r, 3, :, cols] = ot
            minus = -jnp.sum(gf * ot.astype(F32), axis=0, keepdims=True)
            m_high = minus.astype(BF16).astype(F32)
            row = lax.broadcasted_iota(jnp.int32, (PACK, block), 0)
            m_two = jnp.where(row == 0, m_high, jnp.where(row == 1, minus - m_high, 0.0)).astype(BF16)
            g_two = jnp.concatenate([gt, m_two, jnp.zeros((LANES - head_dim - PACK, block), BF16)], 0)
            ds = e * dot(vv[...], g_two, 1, 0).astype(BF16)
            res[r, 0, :, cols] = (dot(kt, ds, 1, 0) * (inv * scale)).astype(BF16)
            qs = (qt * (inv * scale)).astype(BF16)
            gs = (gf * inv).astype(BF16)
            zero = jnp.zeros((head_dim, block), BF16)
            right = jnp.concatenate(
                [
                    jnp.concatenate([gs, zero], 1),
                    jnp.concatenate([zero, qs], 1),
                    jnp.zeros((LANES - 2 * head_dim, 2 * block), BF16),
                ],
                0,
            )
            acc[...] += dot(jnp.concatenate([e, ds], 1), right, 1, 1)
            return inner

        lax.fori_loop(0, seg // block, q_block, 0)

        @pl.when(r >= rounds - 2)
        def _():
            send_attn(r)

        t = acc[...].astype(BF16).T
        res[r, 2] = t[:head_dim]
        res[r, 1] = t[head_dim : 2 * head_dim]

        @pl.when(r == rounds - 2)
        def _():
            send_grad(0, 2)

        return carry

    lax.fori_loop(0, rounds, attend, 0)
    later = [(r, a) for r in range(rounds) for a in range(3)][3:]
    for piece in later[:3]:
        send_grad(*piece)

    term[...] = jnp.zeros_like(term)

    def finish(r, carry):
        pltpu.make_async_copy(ret.at[r, 3], ret.at[r, 3], attn_recv.at[r]).wait()
        for h in range(heads):
            chosen = x[r, :, h * PACK : (h + 1) * PACK, :].reshape(rows, width)
            here = pl.ds(h * head_dim, head_dim)
            term[here, :] += dot(ret[r, 3, h], chosen, 1, 0)
        return carry

    lax.fori_loop(0, rounds, finish, 0)
    part[...] = term[...].T.reshape(groups, chips, 2, own, width)
    half[...] = part[...].astype(BF16)
    pair = pltpu.make_async_remote_copy(
        src_ref=half.at[:, :, 1 - core],
        dst_ref=pair_in,
        send_sem=pair_send,
        recv_sem=pair_recv,
        device_id={"tok": me + 1 - 2 * core},
        device_id_type=MESH,
    )

    def near(s):
        return pltpu.make_async_remote_copy(
            src_ref=near_out.at[:, flip_bits(chip, s)],
            dst_ref=landed.at[chip],
            send_sem=red_send.at[s],
            recv_sem=red_recv.at[s],
            device_id={"tok": hi * group + flip_bits(chip, s) * 2 + core},
            device_id_type=MESH,
        )

    def far(s):
        return pltpu.make_async_remote_copy(
            src_ref=cross_out.at[flip_bits(hi, s)],
            dst_ref=cross_in.at[hi],
            send_sem=cross_send.at[s],
            recv_sem=cross_recv.at[s],
            device_id={"tok": flip_bits(hi, s) * group + lo},
            device_id_type=MESH,
        )

    def lay_out(r):
        for a, ref in enumerate((dq_hbm, dk_hbm, dv_hbm)):
            pltpu.make_async_copy(ret.at[r, a], ret.at[r, a], ret_recv.at[r, a]).wait()
            laid[r, a] = ret[r, a].reshape(width, rows).T
            pltpu.make_async_copy(laid.at[r, a], ref.at[r], out_sem.at[r, a]).start()

    pair.start()
    for piece in later[3:6]:
        send_grad(*piece)
    pair.wait()
    for j in range(groups):
        for u in range(chips):
            near_out[j, u] = (part[j, u, core] + pair_in[j, u].astype(F32)).astype(BF16)
        mine[j] = part[j, chip, core] + pair_in[j, chip].astype(F32)
    beside = later[6:9]
    for s in range(1, chips):
        near(s).start()
        for piece in beside[(s - 1) * len(beside) // (chips - 1) : s * len(beside) // (chips - 1)]:
            send_grad(*piece)
    for piece in later[9:9]:
        send_grad(*piece)
    lay_out(0)
    for s in range(1, chips):
        near(s).wait()
    for j in range(groups):
        total = mine[j]
        for s in range(1, chips):
            total = total + landed[flip_bits(chip, s), j].astype(F32)
        mine[j] = total
        cross_out[j] = total.astype(BF16)
    for s in range(1, groups):
        far(s).start()
    for piece in later[9:]:
        send_grad(*piece)
    for r in range(1, rounds - 1):
        lay_out(r)
    for s in range(1, groups):
        far(s).wait()
    total = mine[hi]
    for s in range(1, groups):
        total = total + cross_in[flip_bits(hi, s)].astype(F32)
    gw[...] = total
    pltpu.make_async_copy(gw, gw_hbm, gw_sem).start()
    lay_out(rounds - 1)

    for r in range(rounds):
        blocks = pl.ds(0, heads - 1)
        sent = out_t.at[r, pl.ds(0, 3), blocks]
        pltpu.make_async_copy(sent, sent, qkv_send.at[r]).wait()
        sent = out_t.at[r, 3, blocks]
        pltpu.make_async_copy(sent, sent, g_send.at[r]).wait()
        for a in range(3):
            sent = ret.at[r, a, blocks]
            pltpu.make_async_copy(sent, sent, res_send.at[r, a]).wait()
        sent = ret.at[r, 3, blocks]
        pltpu.make_async_copy(sent, sent, attn_send.at[r]).wait()
    for r in range(rounds):
        for a, ref in enumerate((dq_hbm, dk_hbm, dv_hbm)):
            pltpu.make_async_copy(laid.at[r, a], ref.at[r], out_sem.at[r, a]).wait()
    pltpu.make_async_copy(gw, gw_hbm, gw_sem).wait()


def hand_over(*refs):
    count = (len(refs) - 2) // 3
    got, given, kept = refs[:count], refs[count : 2 * count], refs[2 * count : 3 * count]
    in_sem, out_sem = refs[3 * count :]
    into = [pltpu.make_async_copy(got[i], kept[i], in_sem.at[i]) for i in range(count)]
    out_of = [pltpu.make_async_copy(kept[i], given[i], out_sem.at[i]) for i in range(count)]
    for copy in into:
        copy.start()
    for i in range(count):
        into[i].wait()
        out_of[i].start()
    for copy in out_of:
        copy.wait()


def local(queries, key_rows, value_rows, projected_output_gradient, out_weight, offsets):
    rounds, rows, width = queries.shape
    heads = offsets.shape[0]
    head_dim = width // heads
    tok = lax.axis_size("tok")
    phases = projected_output_gradient.shape[1] // rows
    seg = heads * rows
    own = width // tok
    group = heads // 2
    groups = tok // group
    dims = (rounds, rows, width, heads, head_dim, tok, phases)
    tokens = projected_output_gradient.reshape(rounds, rows // PACK, PACK * phases, width)
    hbm = pl.BlockSpec(memory_space=pl.ANY)
    rows_shape = jax.ShapeDtypeStruct((rounds, rows, width), BF16)
    out_shape = (rows_shape, rows_shape, rows_shape, jax.ShapeDtypeStruct((own, width), F32))
    dma = pltpu.SemaphoreType.DMA
    results = pl.pallas_call(
        functools.partial(main_kernel, dims),
        out_shape=out_shape,
        in_specs=[pl.BlockSpec(memory_space=pltpu.SMEM)] + [hbm] * 5,
        out_specs=(hbm,) * 4,
        scratch_shapes=[
            pltpu.VMEM((rounds, rows // PACK, PACK * phases, width), BF16),
            pltpu.VMEM((rounds, 3, rows, width), BF16),
            pltpu.VMEM((width, width), BF16),
            pltpu.VMEM((width, width), BF16),
            pltpu.VMEM((PACK * heads, PACK * phases), BF16),
            pltpu.VMEM((rounds, 4, heads, head_dim, rows), BF16),
            pltpu.VMEM((rounds, 4, head_dim, seg), BF16),
            pltpu.VMEM((rounds, 4, head_dim, seg), BF16),
            pltpu.VMEM((rounds, 4, heads, head_dim, rows), BF16),
            pltpu.VMEM((seg, LANES), BF16),
            pltpu.VMEM((seg, LANES), BF16),
            pltpu.VMEM((head_dim + PACK, seg), BF16),
            pltpu.VMEM((seg, LANES), F32),
            pltpu.VMEM((width, width), F32),
            pltpu.VMEM((groups, group // 2, 2, own, width), F32),
            pltpu.VMEM((groups, group // 2, 2, own, width), BF16),
            pltpu.VMEM((groups, group // 2, own, width), BF16),
            pltpu.VMEM((groups, group // 2, own, width), BF16),
            pltpu.VMEM((group // 2, groups, own, width), BF16),
            pltpu.VMEM((groups, own, width), BF16),
            pltpu.VMEM((groups, own, width), BF16),
            pltpu.VMEM((groups, own, width), F32),
            pltpu.VMEM((rounds, 3, rows, width), BF16),
            pltpu.VMEM((own, width), F32),
            dma((rounds,)),
            dma((rounds, 3)),
            dma,
            dma((rounds,)),
            dma((rounds,)),
            dma((rounds,)),
            dma((rounds,)),
            dma((rounds, 3)),
            dma((rounds, 3)),
            dma((rounds,)),
            dma((rounds,)),
            dma,
            dma,
            dma((group // 2,)),
            dma((group // 2,)),
            dma((groups,)),
            dma((groups,)),
            dma((rounds, 3)),
            dma,
        ],
        compiler_params=pltpu.CompilerParams(
            collective_id=0, has_side_effects=True, vmem_limit_bytes=66000000
        ),
        name="branch_backward",
    )(offsets, queries, key_rows, value_rows, out_weight, tokens)
    return pl.pallas_call(
        hand_over,
        out_shape=out_shape,
        in_specs=[hbm] * 4,
        out_specs=(hbm,) * 4,
        scratch_shapes=[pltpu.VMEM(a.shape, a.dtype) for a in out_shape] + [dma((4,)), dma((4,))],
        name="hand_over",
    )(*results)


def solution(mesh):
    placed = (
        P("slides", "tok", None),
        P("slides", "tok", None),
        P("slides", "tok", None),
        P("slides", "tok", None),
        P(),
        P(),
    )
    return jax.shard_map(
        local,
        mesh=mesh,
        in_specs=placed,
        out_specs=(
            P("slides", "tok", None),
            P("slides", "tok", None),
            P("slides", "tok", None),
            P(("slides", "tok"), None),
        ),
        check_vma=False,
    )
```

```python
import functools

import jax
import jax.numpy as jnp
from jax import lax
from jax.experimental import pallas as pl
from jax.experimental.pallas import tpu as pltpu
from jax.sharding import PartitionSpec as P

MESH = pl.DeviceIdType.MESH
F32 = jnp.float32
BF16 = jnp.bfloat16
LOG2E = 1.4426950408889634
LANES = 128
PACK = 16


def dot(a, b, ca, cb):
    return lax.dot_general(a, b, (((ca,), (cb,)), ((), ())), preferred_element_type=F32)


def flip_bits(index, mask):
    out = index
    bit = 1
    while bit <= mask:
        if mask & bit:
            out = out + bit - 2 * bit * ((index // bit) % 2)
        bit *= 2
    return out


def main_kernel(
    dims,
    off_ref, q_hbm, k_hbm, v_hbm, w_hbm, x_hbm,
    dq_hbm, dk_hbm, dv_hbm, gw_hbm,
    x, qkv, w, wt, perm, out_t, recv, res, ret, kk, vv, vt1, acc, term, part, half, pair_in, near_out, landed, cross_out, cross_in, mine,
    laid, gw,
    x_sem, in_sem, w_sem, qkv_send, qkv_recv, g_send, g_recv, res_send, ret_recv, attn_send, attn_recv,
    pair_send, pair_recv, red_send, red_recv, cross_send, cross_recv, out_sem, gw_sem,
):
    rounds, rows, width, heads, head_dim, tok, phases = dims
    seg = heads * rows
    me = lax.axis_index("tok")
    lane = me % heads
    base = me - lane
    order = sorted(range(1, heads), key=lambda s: (-(s // (heads // 2)), -s))
    across = [s for s in order if s >= heads // 2]
    within = [s for s in order if s < heads // 2]
    quarter = lane // (heads // 4)
    outer = jnp.logical_or(quarter == 0, quarter == 3)
    inner = jnp.logical_not(outer)
    scale = head_dim ** (-0.5)
    group = heads // 2
    groups = tok // group
    lo = me % group
    hi = me // group
    chip = lo // 2
    core = lo % 2
    chips = group // 2
    own = width // tok
    chunks = rows // PACK

    greet = sorted(set(range(1, heads)) | set(group * s for s in range(1, groups)))
    barrier = pltpu.get_barrier_semaphore()
    for s in greet:
        pl.semaphore_signal(barrier, inc=1, device_id={"tok": flip_bits(me, s)}, device_id_type=MESH)

    def load_qkv(r):
        return [
            pltpu.make_async_copy(ref.at[r], qkv.at[r, a], in_sem.at[r, a])
            for a, ref in enumerate((q_hbm, k_hbm, v_hbm))
        ]

    def load_x(r):
        return pltpu.make_async_copy(x_hbm.at[r], x.at[r], x_sem.at[r])

    load_w = pltpu.make_async_copy(w_hbm, w, w_sem)
    for r in range(rounds):
        for copy in load_qkv(r):
            copy.start()
        if r == 0:
            load_w.start()
        load_x(r).start()

    def columns(d):
        return pl.ds(pl.multiple_of(d * rows, rows), rows)

    def send_to(peers, r, first, count, send_sem, recv_sem):
        for s in peers:
            d = flip_bits(lane, s)
            pltpu.make_async_remote_copy(
                src_ref=out_t.at[r, pl.ds(first, count), d],
                dst_ref=recv.at[r, pl.ds(first, count), :, columns(lane)],
                send_sem=send_sem.at[r],
                recv_sem=recv_sem.at[r],
                device_id={"tok": base + d},
                device_id_type=MESH,
            ).start()

    def send_across(r, first, count, send_sem, recv_sem):
        send_to(across, r, first, count, send_sem, recv_sem)

    def send_within(r, first, count, send_sem, recv_sem):
        send_to(within, r, first, count, send_sem, recv_sem)
        pltpu.make_async_copy(
            out_t.at[r, pl.ds(first, count), lane],
            recv.at[r, pl.ds(first, count), :, columns(lane)],
            recv_sem.at[r],
        ).start()

    def turn(r):
        for a, copy in enumerate(load_qkv(r)):
            copy.wait()
            out_t[r, a] = qkv[r, a].T.reshape(heads, head_dim, rows)

    def project(r):
        load_x(r).wait()

        def chunk(c, inner):
            x[r, c] = dot(perm[...], x[r, c], 1, 0).astype(BF16)
            return inner

        lax.fori_loop(0, chunks, chunk, 0)
        for h in range(heads):
            chosen = x[r, :, h * PACK : (h + 1) * PACK, :].reshape(rows, width)
            out_t[r, 3, h] = dot(wt[h * head_dim : (h + 1) * head_dim, :], chosen, 1, 1).astype(BF16)

    at = lax.broadcasted_iota(jnp.int32, (PACK, PACK * phases), 1)
    at = at - phases * lax.broadcasted_iota(jnp.int32, (PACK, PACK * phases), 0)
    for h in range(heads):
        perm[h * PACK : (h + 1) * PACK, :] = jnp.where(at == off_ref[h], 1.0, 0.0).astype(BF16)
    for a, copy in enumerate(load_qkv(0)):
        copy.wait()
        out_t[0, a] = qkv[0, a].T.reshape(heads, head_dim, rows)
        if a == 0:
            pl.semaphore_wait(barrier, len(greet))

        @pl.when(outer)
        def _():
            send_across(0, a, 1, qkv_send, qkv_recv)

        send_within(0, a, 1, qkv_send, qkv_recv)

        @pl.when(inner)
        def _():
            send_across(0, a, 1, qkv_send, qkv_recv)

    load_w.wait()
    wt[...] = w[...].T

    def prepare(r, carry):
        project(r)

        @pl.when(jnp.logical_and(r == 0, outer))
        def _():
            send_across(r, 3, 1, g_send, g_recv)

        send_within(r, 3, 1, g_send, g_recv)

        @pl.when(inner)
        def _():
            send_across(r, 3, 1, g_send, g_recv)

        @pl.when(r + 1 < rounds)
        def _():
            turn(r + 1)
            send_within(r + 1, 0, 3, qkv_send, qkv_recv)

            @pl.when(inner)
            def _():
                send_across(r + 1, 0, 3, qkv_send, qkv_recv)

        return carry

    lax.fori_loop(0, rounds, prepare, 0)

    def send_back(r, a, send_sem, recv_sem):
        def send_to_all(peers):
            for s in peers:
                d = flip_bits(lane, s)
                pltpu.make_async_remote_copy(
                    src_ref=res.at[r, a, :, columns(d)],
                    dst_ref=ret.at[r, a, lane],
                    send_sem=send_sem,
                    recv_sem=recv_sem,
                    device_id={"tok": base + d},
                    device_id_type=MESH,
                ).start()

        @pl.when(outer)
        def _():
            send_to_all(across)

        send_to_all(within)
        pltpu.make_async_copy(res.at[r, a, :, columns(lane)], ret.at[r, a, lane], recv_sem).start()

        @pl.when(inner)
        def _():
            send_to_all(across)

    def send_attn(r):
        send_back(r, 3, attn_send.at[r], attn_recv.at[r])

    def send_grad(r, a):
        send_back(r, a, res_send.at[r, a], ret_recv.at[r, a])

    block = seg // 2
    k_pad = jnp.zeros((LANES - 2 * head_dim, seg), BF16)
    v_pad = jnp.zeros((LANES - head_dim - PACK, seg), BF16)
    ones = jnp.ones((PACK, seg), BF16)

    def attend(r, carry):
        got = recv.at[r, pl.ds(0, 3)]
        pltpu.make_async_copy(got, got, qkv_recv.at[r]).wait()
        pltpu.make_async_copy(recv.at[r, 3], recv.at[r, 3], g_recv.at[r]).wait()

        @pl.when(jnp.logical_and(outer, r + 1 < rounds))
        def _():
            send_across(r + 1, 0, 3, qkv_send, qkv_recv)
            send_across(r + 1, 3, 1, g_send, g_recv)

        @pl.when(r == rounds - 2)
        def _():
            def one(i, inner_carry):
                send_attn(i)
                return inner_carry

            lax.fori_loop(0, rounds - 2, one, 0)
            send_grad(0, 0)
            send_grad(0, 1)
            send_grad(0, 2)

        kt = recv[r, 1]
        vt = recv[r, 2]
        kk[...] = jnp.concatenate([kt, kt, k_pad], 0).T
        vv[...] = jnp.concatenate([vt, ones, v_pad], 0).T
        vt1[...] = jnp.concatenate([vt, ones], 0)
        acc[...] = jnp.zeros_like(acc)
        def q_block(b, inner):
            cols = pl.ds(pl.multiple_of(b * block, block), block)
            qt = recv[r, 0, :, cols].astype(F32)
            gt = recv[r, 3, :, cols]
            gf = gt.astype(F32)
            qc = qt * (scale * LOG2E)
            q_high = qc.astype(BF16)
            q_low = (qc - q_high.astype(F32)).astype(BF16)
            q_two = jnp.concatenate([q_high, q_low, jnp.zeros((LANES - 2 * head_dim, block), BF16)], 0)
            s = dot(kk[...], q_two, 1, 0)
            e = jnp.exp2(s - jnp.max(s, axis=0, keepdims=True)).astype(BF16)
            both = dot(vt1[...], e, 1, 0)
            inv = 1.0 / both[head_dim : head_dim + 1]
            ot = (both[:head_dim] * inv).astype(BF16)
            res[r, 3, :, cols] = ot
            minus = -jnp.sum(gf * ot.astype(F32), axis=0, keepdims=True)
            m_high = minus.astype(BF16).astype(F32)
            row = lax.broadcasted_iota(jnp.int32, (PACK, block), 0)
            m_two = jnp.where(row == 0, m_high, jnp.where(row == 1, minus - m_high, 0.0)).astype(BF16)
            g_two = jnp.concatenate([gt, m_two, jnp.zeros((LANES - head_dim - PACK, block), BF16)], 0)
            ds = e * dot(vv[...], g_two, 1, 0).astype(BF16)
            res[r, 0, :, cols] = (dot(kt, ds, 1, 0) * (inv * scale)).astype(BF16)
            qs = (qt * (inv * scale)).astype(BF16)
            gs = (gf * inv).astype(BF16)
            zero = jnp.zeros((head_dim, block), BF16)
            right = jnp.concatenate(
                [
                    jnp.concatenate([gs, zero], 1),
                    jnp.concatenate([zero, qs], 1),
                    jnp.zeros((LANES - 2 * head_dim, 2 * block), BF16),
                ],
                0,
            )
            acc[...] += dot(jnp.concatenate([e, ds], 1), right, 1, 1)
            return inner

        lax.fori_loop(0, seg // block, q_block, 0)

        @pl.when(r >= rounds - 2)
        def _():
            send_attn(r)

        t = acc[...].astype(BF16).T
        res[r, 2] = t[:head_dim]
        res[r, 1] = t[head_dim : 2 * head_dim]

        @pl.when(r == rounds - 2)
        def _():
            send_grad(1, 0)
            send_grad(1, 1)

        return carry

    lax.fori_loop(0, rounds, attend, 0)
    later = [(r, a) for r in range(rounds) for a in range(3)][5:]
    for piece in later[:2]:
        send_grad(*piece)

    term[...] = jnp.zeros_like(term)

    def finish(r, carry):
        pltpu.make_async_copy(ret.at[r, 3], ret.at[r, 3], attn_recv.at[r]).wait()
        for h in range(heads):
            chosen = x[r, :, h * PACK : (h + 1) * PACK, :].reshape(rows, width)
            here = pl.ds(h * head_dim, head_dim)
            term[here, :] += dot(ret[r, 3, h], chosen, 1, 0)
        return carry

    lax.fori_loop(0, rounds, finish, 0)
    part[...] = term[...].T.reshape(groups, chips, 2, own, width)
    half[...] = part[...].astype(BF16)
    pair = pltpu.make_async_remote_copy(
        src_ref=half.at[:, :, 1 - core],
        dst_ref=pair_in,
        send_sem=pair_send,
        recv_sem=pair_recv,
        device_id={"tok": me + 1 - 2 * core},
        device_id_type=MESH,
    )

    def near(s):
        return pltpu.make_async_remote_copy(
            src_ref=near_out.at[:, flip_bits(chip, s)],
            dst_ref=landed.at[chip],
            send_sem=red_send.at[s],
            recv_sem=red_recv.at[s],
            device_id={"tok": hi * group + flip_bits(chip, s) * 2 + core},
            device_id_type=MESH,
        )

    def far(s):
        return pltpu.make_async_remote_copy(
            src_ref=cross_out.at[flip_bits(hi, s)],
            dst_ref=cross_in.at[hi],
            send_sem=cross_send.at[s],
            recv_sem=cross_recv.at[s],
            device_id={"tok": flip_bits(hi, s) * group + lo},
            device_id_type=MESH,
        )

    def lay_out(r):
        for a, ref in enumerate((dq_hbm, dk_hbm, dv_hbm)):
            pltpu.make_async_copy(ret.at[r, a], ret.at[r, a], ret_recv.at[r, a]).wait()
            laid[r, a] = ret[r, a].reshape(width, rows).T
            pltpu.make_async_copy(laid.at[r, a], ref.at[r], out_sem.at[r, a]).start()

    pair.start()
    for piece in later[2:4]:
        send_grad(*piece)
    pair.wait()
    for j in range(groups):
        for u in range(chips):
            near_out[j, u] = (part[j, u, core] + pair_in[j, u].astype(F32)).astype(BF16)
        mine[j] = part[j, chip, core] + pair_in[j, chip].astype(F32)
    beside = later[4:7]
    for s in range(1, chips):
        near(s).start()
        for piece in beside[(s - 1) * len(beside) // (chips - 1) : s * len(beside) // (chips - 1)]:
            send_grad(*piece)
    for piece in later[7:7]:
        send_grad(*piece)
    lay_out(0)
    for s in range(1, chips):
        near(s).wait()
    for j in range(groups):
        total = mine[j]
        for s in range(1, chips):
            total = total + landed[flip_bits(chip, s), j].astype(F32)
        mine[j] = total
        cross_out[j] = total.astype(BF16)
    for s in range(1, groups):
        far(s).start()
    for piece in later[7:]:
        send_grad(*piece)
    for r in range(1, rounds - 1):
        lay_out(r)
    for s in range(1, groups):
        far(s).wait()
    total = mine[hi]
    for s in range(1, groups):
        total = total + cross_in[flip_bits(hi, s)].astype(F32)
    gw[...] = total
    pltpu.make_async_copy(gw, gw_hbm, gw_sem).start()
    lay_out(rounds - 1)

    for r in range(rounds):
        blocks = pl.ds(0, heads - 1)
        sent = out_t.at[r, pl.ds(0, 3), blocks]
        pltpu.make_async_copy(sent, sent, qkv_send.at[r]).wait()
        sent = out_t.at[r, 3, blocks]
        pltpu.make_async_copy(sent, sent, g_send.at[r]).wait()
        for a in range(3):
            sent = ret.at[r, a, blocks]
            pltpu.make_async_copy(sent, sent, res_send.at[r, a]).wait()
        sent = ret.at[r, 3, blocks]
        pltpu.make_async_copy(sent, sent, attn_send.at[r]).wait()
    for r in range(rounds):
        for a, ref in enumerate((dq_hbm, dk_hbm, dv_hbm)):
            pltpu.make_async_copy(laid.at[r, a], ref.at[r], out_sem.at[r, a]).wait()
    pltpu.make_async_copy(gw, gw_hbm, gw_sem).wait()


def hand_over(*refs):
    count = (len(refs) - 2) // 3
    got, given, kept = refs[:count], refs[count : 2 * count], refs[2 * count : 3 * count]
    in_sem, out_sem = refs[3 * count :]
    pieces = [(i, r) for r in range(got[0].shape[0]) for i in range(count - 1)] + [(count - 1, None)]

    def both(n, i, r):
        a, b, c = (got[i], given[i], kept[i]) if r is None else (got[i].at[r], given[i].at[r], kept[i].at[r])
        return pltpu.make_async_copy(a, c, in_sem.at[n]), pltpu.make_async_copy(c, b, out_sem.at[n])

    copies = [both(n, i, r) for n, (i, r) in enumerate(pieces)]
    for into, _ in copies:
        into.start()
    for into, out_of in copies:
        into.wait()
        out_of.start()
    for _, out_of in copies:
        out_of.wait()


def local(queries, key_rows, value_rows, projected_output_gradient, out_weight, offsets):
    rounds, rows, width = queries.shape
    heads = offsets.shape[0]
    head_dim = width // heads
    tok = lax.axis_size("tok")
    phases = projected_output_gradient.shape[1] // rows
    seg = heads * rows
    own = width // tok
    group = heads // 2
    groups = tok // group
    dims = (rounds, rows, width, heads, head_dim, tok, phases)
    tokens = projected_output_gradient.reshape(rounds, rows // PACK, PACK * phases, width)
    hbm = pl.BlockSpec(memory_space=pl.ANY)
    rows_shape = jax.ShapeDtypeStruct((rounds, rows, width), BF16)
    out_shape = (rows_shape, rows_shape, rows_shape, jax.ShapeDtypeStruct((own, width), F32))
    dma = pltpu.SemaphoreType.DMA
    results = pl.pallas_call(
        functools.partial(main_kernel, dims),
        out_shape=out_shape,
        in_specs=[pl.BlockSpec(memory_space=pltpu.SMEM)] + [hbm] * 5,
        out_specs=(hbm,) * 4,
        scratch_shapes=[
            pltpu.VMEM((rounds, rows // PACK, PACK * phases, width), BF16),
            pltpu.VMEM((rounds, 3, rows, width), BF16),
            pltpu.VMEM((width, width), BF16),
            pltpu.VMEM((width, width), BF16),
            pltpu.VMEM((PACK * heads, PACK * phases), BF16),
            pltpu.VMEM((rounds, 4, heads, head_dim, rows), BF16),
            pltpu.VMEM((rounds, 4, head_dim, seg), BF16),
            pltpu.VMEM((rounds, 4, head_dim, seg), BF16),
            pltpu.VMEM((rounds, 4, heads, head_dim, rows), BF16),
            pltpu.VMEM((seg, LANES), BF16),
            pltpu.VMEM((seg, LANES), BF16),
            pltpu.VMEM((head_dim + PACK, seg), BF16),
            pltpu.VMEM((seg, LANES), F32),
            pltpu.VMEM((width, width), F32),
            pltpu.VMEM((groups, group // 2, 2, own, width), F32),
            pltpu.VMEM((groups, group // 2, 2, own, width), BF16),
            pltpu.VMEM((groups, group // 2, own, width), BF16),
            pltpu.VMEM((groups, group // 2, own, width), BF16),
            pltpu.VMEM((group // 2, groups, own, width), BF16),
            pltpu.VMEM((groups, own, width), BF16),
            pltpu.VMEM((groups, own, width), BF16),
            pltpu.VMEM((groups, own, width), F32),
            pltpu.VMEM((rounds, 3, rows, width), BF16),
            pltpu.VMEM((own, width), F32),
            dma((rounds,)),
            dma((rounds, 3)),
            dma,
            dma((rounds,)),
            dma((rounds,)),
            dma((rounds,)),
            dma((rounds,)),
            dma((rounds, 3)),
            dma((rounds, 3)),
            dma((rounds,)),
            dma((rounds,)),
            dma,
            dma,
            dma((group // 2,)),
            dma((group // 2,)),
            dma((groups,)),
            dma((groups,)),
            dma((rounds, 3)),
            dma,
        ],
        compiler_params=pltpu.CompilerParams(
            collective_id=0, has_side_effects=True, vmem_limit_bytes=66000000
        ),
        name="branch_backward",
    )(offsets, queries, key_rows, value_rows, out_weight, tokens)
    return pl.pallas_call(
        hand_over,
        out_shape=out_shape,
        in_specs=[hbm] * 4,
        out_specs=(hbm,) * 4,
        scratch_shapes=[pltpu.VMEM(a.shape, a.dtype) for a in out_shape] + [dma((3 * rounds + 1,)), dma((3 * rounds + 1,))],
        name="hand_over",
    )(*results)


def solution(mesh):
    placed = (
        P("slides", "tok", None),
        P("slides", "tok", None),
        P("slides", "tok", None),
        P("slides", "tok", None),
        P(),
        P(),
    )
    return jax.shard_map(
        local,
        mesh=mesh,
        in_specs=placed,
        out_specs=(
            P("slides", "tok", None),
            P("slides", "tok", None),
            P("slides", "tok", None),
            P(("slides", "tok"), None),
        ),
        check_vma=False,
    )
```

```python
import functools

import jax
import jax.numpy as jnp
from jax import lax
from jax.experimental import pallas as pl
from jax.experimental.pallas import tpu as pltpu
from jax.sharding import PartitionSpec as P

MESH = pl.DeviceIdType.MESH
F32 = jnp.float32
BF16 = jnp.bfloat16
LOG2E = 1.4426950408889634
LANES = 128
PACK = 16


def dot(a, b, ca, cb):
    return lax.dot_general(a, b, (((ca,), (cb,)), ((), ())), preferred_element_type=F32)


def flip_bits(index, mask):
    out = index
    bit = 1
    while bit <= mask:
        if mask & bit:
            out = out + bit - 2 * bit * ((index // bit) % 2)
        bit *= 2
    return out


def main_kernel(
    dims,
    off_ref, q_hbm, k_hbm, v_hbm, w_hbm, x_hbm,
    dq_hbm, dk_hbm, dv_hbm, gw_hbm,
    x, qkv, w, wt, perm, out_t, recv, res, ret, kk, vv, vt1, acc, term, part, half, pair_in, near_out, landed, cross_out, cross_in, mine,
    laid, gw,
    x_sem, in_sem, w_sem, qkv_send, qkv_recv, g_send, g_recv, res_send, ret_recv, attn_send, attn_recv,
    pair_send, pair_recv, red_send, red_recv, cross_send, cross_recv, out_sem, gw_sem,
):
    rounds, rows, width, heads, head_dim, tok, phases = dims
    seg = heads * rows
    me = lax.axis_index("tok")
    lane = me % heads
    base = me - lane
    order = sorted(range(1, heads), key=lambda s: (-(s // (heads // 2)), -s))
    across = [s for s in order if s >= heads // 2]
    within = [s for s in order if s < heads // 2]
    quarter = lane // (heads // 4)
    outer = jnp.logical_or(quarter == 0, quarter == 3)
    inner = jnp.logical_not(outer)
    scale = head_dim ** (-0.5)
    group = heads // 2
    groups = tok // group
    lo = me % group
    hi = me // group
    chip = lo // 2
    core = lo % 2
    chips = group // 2
    own = width // tok
    chunks = rows // PACK

    greet = sorted(set(range(1, heads)) | set(group * s for s in range(1, groups)))
    barrier = pltpu.get_barrier_semaphore()
    for s in greet:
        pl.semaphore_signal(barrier, inc=1, device_id={"tok": flip_bits(me, s)}, device_id_type=MESH)

    def load_qkv(r):
        return [
            pltpu.make_async_copy(ref.at[r], qkv.at[r, a], in_sem.at[r, a])
            for a, ref in enumerate((q_hbm, k_hbm, v_hbm))
        ]

    def load_x(r):
        return pltpu.make_async_copy(x_hbm.at[r], x.at[r], x_sem.at[r])

    load_w = pltpu.make_async_copy(w_hbm, w, w_sem)
    for r in range(rounds):
        for copy in load_qkv(r):
            copy.start()
        if r == 0:
            load_w.start()
        load_x(r).start()

    def columns(d):
        return pl.ds(pl.multiple_of(d * rows, rows), rows)

    def send_to(peers, r, first, count, send_sem, recv_sem):
        for s in peers:
            d = flip_bits(lane, s)
            pltpu.make_async_remote_copy(
                src_ref=out_t.at[r, pl.ds(first, count), d],
                dst_ref=recv.at[r, pl.ds(first, count), :, columns(lane)],
                send_sem=send_sem.at[r],
                recv_sem=recv_sem.at[r],
                device_id={"tok": base + d},
                device_id_type=MESH,
            ).start()

    def send_across(r, first, count, send_sem, recv_sem):
        send_to(across, r, first, count, send_sem, recv_sem)

    def send_within(r, first, count, send_sem, recv_sem):
        send_to(within, r, first, count, send_sem, recv_sem)
        pltpu.make_async_copy(
            out_t.at[r, pl.ds(first, count), lane],
            recv.at[r, pl.ds(first, count), :, columns(lane)],
            recv_sem.at[r],
        ).start()

    def turn(r):
        for a, copy in enumerate(load_qkv(r)):
            copy.wait()
            out_t[r, a] = qkv[r, a].T.reshape(heads, head_dim, rows)

    def project(r):
        load_x(r).wait()

        def chunk(c, inner):
            x[r, c] = dot(perm[...], x[r, c], 1, 0).astype(BF16)
            return inner

        lax.fori_loop(0, chunks, chunk, 0)
        for h in range(heads):
            chosen = x[r, :, h * PACK : (h + 1) * PACK, :].reshape(rows, width)
            out_t[r, 3, h] = dot(wt[h * head_dim : (h + 1) * head_dim, :], chosen, 1, 1).astype(BF16)

    at = lax.broadcasted_iota(jnp.int32, (PACK, PACK * phases), 1)
    at = at - phases * lax.broadcasted_iota(jnp.int32, (PACK, PACK * phases), 0)
    for h in range(heads):
        perm[h * PACK : (h + 1) * PACK, :] = jnp.where(at == off_ref[h], 1.0, 0.0).astype(BF16)
    for a, copy in enumerate(load_qkv(0)):
        copy.wait()
        out_t[0, a] = qkv[0, a].T.reshape(heads, head_dim, rows)
        if a == 0:
            pl.semaphore_wait(barrier, len(greet))

        @pl.when(outer)
        def _():
            send_across(0, a, 1, qkv_send, qkv_recv)

        send_within(0, a, 1, qkv_send, qkv_recv)

        @pl.when(inner)
        def _():
            send_across(0, a, 1, qkv_send, qkv_recv)

    load_w.wait()
    wt[...] = w[...].T

    def prepare(r, carry):
        project(r)

        @pl.when(jnp.logical_and(r == 0, outer))
        def _():
            send_across(r, 3, 1, g_send, g_recv)

        send_within(r, 3, 1, g_send, g_recv)

        @pl.when(inner)
        def _():
            send_across(r, 3, 1, g_send, g_recv)

        @pl.when(r + 1 < rounds)
        def _():
            turn(r + 1)
            send_within(r + 1, 0, 3, qkv_send, qkv_recv)

            @pl.when(inner)
            def _():
                send_across(r + 1, 0, 3, qkv_send, qkv_recv)

        return carry

    lax.fori_loop(0, rounds, prepare, 0)

    def send_back(r, a, send_sem, recv_sem):
        def send_to_all(peers):
            for s in peers:
                d = flip_bits(lane, s)
                pltpu.make_async_remote_copy(
                    src_ref=res.at[r, a, :, columns(d)],
                    dst_ref=ret.at[r, a, lane],
                    send_sem=send_sem,
                    recv_sem=recv_sem,
                    device_id={"tok": base + d},
                    device_id_type=MESH,
                ).start()

        @pl.when(outer)
        def _():
            send_to_all(across)

        send_to_all(within)
        pltpu.make_async_copy(res.at[r, a, :, columns(lane)], ret.at[r, a, lane], recv_sem).start()

        @pl.when(inner)
        def _():
            send_to_all(across)

    def send_attn(r):
        send_back(r, 3, attn_send.at[r], attn_recv.at[r])

    def send_grad(r, a):
        send_back(r, a, res_send.at[r, a], ret_recv.at[r, a])

    block = seg // 2
    k_pad = jnp.zeros((LANES - 2 * head_dim, seg), BF16)
    v_pad = jnp.zeros((LANES - head_dim - PACK, seg), BF16)
    ones = jnp.ones((PACK, seg), BF16)

    def attend(r, carry):
        got = recv.at[r, pl.ds(0, 3)]
        pltpu.make_async_copy(got, got, qkv_recv.at[r]).wait()
        pltpu.make_async_copy(recv.at[r, 3], recv.at[r, 3], g_recv.at[r]).wait()

        @pl.when(jnp.logical_and(outer, r + 1 < rounds))
        def _():
            send_across(r + 1, 0, 3, qkv_send, qkv_recv)
            send_across(r + 1, 3, 1, g_send, g_recv)

        @pl.when(r == rounds - 2)
        def _():
            def one(i, inner_carry):
                send_attn(i)
                return inner_carry

            lax.fori_loop(0, rounds - 2, one, 0)
            send_grad(0, 0)
            send_grad(0, 1)
            send_grad(0, 2)

        kt = recv[r, 1]
        vt = recv[r, 2]
        kk[...] = jnp.concatenate([kt, kt, k_pad], 0).T
        vv[...] = jnp.concatenate([vt, ones, v_pad], 0).T
        vt1[...] = jnp.concatenate([vt, ones], 0)
        acc[...] = jnp.zeros_like(acc)
        def q_block(b, inner):
            cols = pl.ds(pl.multiple_of(b * block, block), block)
            qt = recv[r, 0, :, cols].astype(F32)
            gt = recv[r, 3, :, cols]
            gf = gt.astype(F32)
            qc = qt * (scale * LOG2E)
            q_high = qc.astype(BF16)
            q_low = (qc - q_high.astype(F32)).astype(BF16)
            q_two = jnp.concatenate([q_high, q_low, jnp.zeros((LANES - 2 * head_dim, block), BF16)], 0)
            s = dot(kk[...], q_two, 1, 0)
            e = jnp.exp2(s - jnp.max(s, axis=0, keepdims=True)).astype(BF16)
            both = dot(vt1[...], e, 1, 0)
            inv = 1.0 / both[head_dim : head_dim + 1]
            ot = (both[:head_dim] * inv).astype(BF16)
            res[r, 3, :, cols] = ot
            minus = -jnp.sum(gf * ot.astype(F32), axis=0, keepdims=True)
            m_high = minus.astype(BF16).astype(F32)
            row = lax.broadcasted_iota(jnp.int32, (PACK, block), 0)
            m_two = jnp.where(row == 0, m_high, jnp.where(row == 1, minus - m_high, 0.0)).astype(BF16)
            g_two = jnp.concatenate([gt, m_two, jnp.zeros((LANES - head_dim - PACK, block), BF16)], 0)
            ds = e * dot(vv[...], g_two, 1, 0).astype(BF16)
            res[r, 0, :, cols] = (dot(kt, ds, 1, 0) * (inv * scale)).astype(BF16)
            qs = (qt * (inv * scale)).astype(BF16)
            gs = (gf * inv).astype(BF16)
            zero = jnp.zeros((head_dim, block), BF16)
            right = jnp.concatenate(
                [
                    jnp.concatenate([gs, zero], 1),
                    jnp.concatenate([zero, qs], 1),
                    jnp.zeros((LANES - 2 * head_dim, 2 * block), BF16),
                ],
                0,
            )
            acc[...] += dot(jnp.concatenate([e, ds], 1), right, 1, 1)
            return inner

        lax.fori_loop(0, seg // block, q_block, 0)

        @pl.when(r >= rounds - 2)
        def _():
            send_attn(r)

        t = acc[...].astype(BF16).T
        res[r, 2] = t[:head_dim]
        res[r, 1] = t[head_dim : 2 * head_dim]

        @pl.when(r == rounds - 2)
        def _():
            send_grad(1, 0)
            send_grad(1, 1)

        return carry

    lax.fori_loop(0, rounds, attend, 0)
    later = [(r, a) for r in range(rounds) for a in range(3)][5:]
    for piece in later[:2]:
        send_grad(*piece)

    term[...] = jnp.zeros_like(term)

    def finish(r, carry):
        pltpu.make_async_copy(ret.at[r, 3], ret.at[r, 3], attn_recv.at[r]).wait()
        for h in range(heads):
            chosen = x[r, :, h * PACK : (h + 1) * PACK, :].reshape(rows, width)
            here = pl.ds(h * head_dim, head_dim)
            term[here, :] += dot(ret[r, 3, h], chosen, 1, 0)
        return carry

    lax.fori_loop(0, rounds, finish, 0)
    part[...] = term[...].T.reshape(groups, chips, 2, own, width)
    half[...] = part[...].astype(BF16)
    pair = pltpu.make_async_remote_copy(
        src_ref=half.at[:, :, 1 - core],
        dst_ref=pair_in,
        send_sem=pair_send,
        recv_sem=pair_recv,
        device_id={"tok": me + 1 - 2 * core},
        device_id_type=MESH,
    )

    def near(s):
        return pltpu.make_async_remote_copy(
            src_ref=near_out.at[:, flip_bits(chip, s)],
            dst_ref=landed.at[chip],
            send_sem=red_send.at[s],
            recv_sem=red_recv.at[s],
            device_id={"tok": hi * group + flip_bits(chip, s) * 2 + core},
            device_id_type=MESH,
        )

    def far(s):
        return pltpu.make_async_remote_copy(
            src_ref=cross_out.at[flip_bits(hi, s)],
            dst_ref=cross_in.at[hi],
            send_sem=cross_send.at[s],
            recv_sem=cross_recv.at[s],
            device_id={"tok": flip_bits(hi, s) * group + lo},
            device_id_type=MESH,
        )

    def lay_out(r):
        for a, ref in enumerate((dq_hbm, dk_hbm, dv_hbm)):
            pltpu.make_async_copy(ret.at[r, a], ret.at[r, a], ret_recv.at[r, a]).wait()
            laid[r, a] = ret[r, a].reshape(width, rows).T
            pltpu.make_async_copy(laid.at[r, a], ref.at[r], out_sem.at[r, a]).start()

    pair.start()
    for piece in later[2:4]:
        send_grad(*piece)
    pair.wait()
    for j in range(groups):
        for u in range(chips):
            near_out[j, u] = (part[j, u, core] + pair_in[j, u].astype(F32)).astype(BF16)
        mine[j] = part[j, chip, core] + pair_in[j, chip].astype(F32)
    beside = later[4:7]
    for s in range(1, chips):
        near(s).start()
        for piece in beside[(s - 1) * len(beside) // (chips - 1) : s * len(beside) // (chips - 1)]:
            send_grad(*piece)
    for piece in later[7:7]:
        send_grad(*piece)
    lay_out(0)
    for s in range(1, chips):
        near(s).wait()
    for j in range(groups):
        total = mine[j]
        for s in range(1, chips):
            total = total + landed[flip_bits(chip, s), j].astype(F32)
        mine[j] = total
        cross_out[j] = total.astype(BF16)
    for s in range(1, groups):
        far(s).start()
    for piece in later[7:]:
        send_grad(*piece)
    for r in range(1, rounds - 1):
        lay_out(r)
    lay_out(rounds - 1)
    for s in range(1, groups):
        far(s).wait()
    total = mine[hi]
    for s in range(1, groups):
        total = total + cross_in[flip_bits(hi, s)].astype(F32)
    gw[...] = total
    pltpu.make_async_copy(gw, gw_hbm, gw_sem).start()

    for r in range(rounds):
        blocks = pl.ds(0, heads - 1)
        sent = out_t.at[r, pl.ds(0, 3), blocks]
        pltpu.make_async_copy(sent, sent, qkv_send.at[r]).wait()
        sent = out_t.at[r, 3, blocks]
        pltpu.make_async_copy(sent, sent, g_send.at[r]).wait()
        for a in range(3):
            sent = ret.at[r, a, blocks]
            pltpu.make_async_copy(sent, sent, res_send.at[r, a]).wait()
        sent = ret.at[r, 3, blocks]
        pltpu.make_async_copy(sent, sent, attn_send.at[r]).wait()
    for r in range(rounds):
        for a, ref in enumerate((dq_hbm, dk_hbm, dv_hbm)):
            pltpu.make_async_copy(laid.at[r, a], ref.at[r], out_sem.at[r, a]).wait()
    pltpu.make_async_copy(gw, gw_hbm, gw_sem).wait()


def hand_over(*refs):
    count = (len(refs) - 2) // 3
    got, given, kept = refs[:count], refs[count : 2 * count], refs[2 * count : 3 * count]
    in_sem, out_sem = refs[3 * count :]
    pieces = [(i, r) for r in range(got[0].shape[0]) for i in range(count - 1)] + [(count - 1, None)]

    def both(n, i, r):
        a, b, c = (got[i], given[i], kept[i]) if r is None else (got[i].at[r], given[i].at[r], kept[i].at[r])
        return pltpu.make_async_copy(a, c, in_sem.at[n]), pltpu.make_async_copy(c, b, out_sem.at[n])

    copies = [both(n, i, r) for n, (i, r) in enumerate(pieces)]
    for into, _ in copies:
        into.start()
    for into, out_of in copies:
        into.wait()
        out_of.start()
    for _, out_of in copies:
        out_of.wait()


def local(queries, key_rows, value_rows, projected_output_gradient, out_weight, offsets):
    rounds, rows, width = queries.shape
    heads = offsets.shape[0]
    head_dim = width // heads
    tok = lax.axis_size("tok")
    phases = projected_output_gradient.shape[1] // rows
    seg = heads * rows
    own = width // tok
    group = heads // 2
    groups = tok // group
    dims = (rounds, rows, width, heads, head_dim, tok, phases)
    tokens = projected_output_gradient.reshape(rounds, rows // PACK, PACK * phases, width)
    hbm = pl.BlockSpec(memory_space=pl.ANY)
    rows_shape = jax.ShapeDtypeStruct((rounds, rows, width), BF16)
    out_shape = (rows_shape, rows_shape, rows_shape, jax.ShapeDtypeStruct((own, width), F32))
    dma = pltpu.SemaphoreType.DMA
    results = pl.pallas_call(
        functools.partial(main_kernel, dims),
        out_shape=out_shape,
        in_specs=[pl.BlockSpec(memory_space=pltpu.SMEM)] + [hbm] * 5,
        out_specs=(hbm,) * 4,
        scratch_shapes=[
            pltpu.VMEM((rounds, rows // PACK, PACK * phases, width), BF16),
            pltpu.VMEM((rounds, 3, rows, width), BF16),
            pltpu.VMEM((width, width), BF16),
            pltpu.VMEM((width, width), BF16),
            pltpu.VMEM((PACK * heads, PACK * phases), BF16),
            pltpu.VMEM((rounds, 4, heads, head_dim, rows), BF16),
            pltpu.VMEM((rounds, 4, head_dim, seg), BF16),
            pltpu.VMEM((rounds, 4, head_dim, seg), BF16),
            pltpu.VMEM((rounds, 4, heads, head_dim, rows), BF16),
            pltpu.VMEM((seg, LANES), BF16),
            pltpu.VMEM((seg, LANES), BF16),
            pltpu.VMEM((head_dim + PACK, seg), BF16),
            pltpu.VMEM((seg, LANES), F32),
            pltpu.VMEM((width, width), F32),
            pltpu.VMEM((groups, group // 2, 2, own, width), F32),
            pltpu.VMEM((groups, group // 2, 2, own, width), BF16),
            pltpu.VMEM((groups, group // 2, own, width), BF16),
            pltpu.VMEM((groups, group // 2, own, width), BF16),
            pltpu.VMEM((group // 2, groups, own, width), BF16),
            pltpu.VMEM((groups, own, width), BF16),
            pltpu.VMEM((groups, own, width), BF16),
            pltpu.VMEM((groups, own, width), F32),
            pltpu.VMEM((rounds, 3, rows, width), BF16),
            pltpu.VMEM((own, width), F32),
            dma((rounds,)),
            dma((rounds, 3)),
            dma,
            dma((rounds,)),
            dma((rounds,)),
            dma((rounds,)),
            dma((rounds,)),
            dma((rounds, 3)),
            dma((rounds, 3)),
            dma((rounds,)),
            dma((rounds,)),
            dma,
            dma,
            dma((group // 2,)),
            dma((group // 2,)),
            dma((groups,)),
            dma((groups,)),
            dma((rounds, 3)),
            dma,
        ],
        compiler_params=pltpu.CompilerParams(
            collective_id=0, has_side_effects=True, vmem_limit_bytes=66000000
        ),
        name="branch_backward",
    )(offsets, queries, key_rows, value_rows, out_weight, tokens)
    return pl.pallas_call(
        hand_over,
        out_shape=out_shape,
        in_specs=[hbm] * 4,
        out_specs=(hbm,) * 4,
        scratch_shapes=[pltpu.VMEM(a.shape, a.dtype) for a in out_shape] + [dma((3 * rounds + 1,)), dma((3 * rounds + 1,))],
        name="hand_over",
    )(*results)


def solution(mesh):
    placed = (
        P("slides", "tok", None),
        P("slides", "tok", None),
        P("slides", "tok", None),
        P("slides", "tok", None),
        P(),
        P(),
    )
    return jax.shard_map(
        local,
        mesh=mesh,
        in_specs=placed,
        out_specs=(
            P("slides", "tok", None),
            P("slides", "tok", None),
            P("slides", "tok", None),
            P(("slides", "tok"), None),
        ),
        check_vma=False,
    )
```

```python
import functools

import jax
import jax.numpy as jnp
from jax import lax
from jax.experimental import pallas as pl
from jax.experimental.pallas import tpu as pltpu
from jax.sharding import PartitionSpec as P

MESH = pl.DeviceIdType.MESH
F32 = jnp.float32
BF16 = jnp.bfloat16
LOG2E = 1.4426950408889634
LANES = 128
PACK = 16


def dot(a, b, ca, cb):
    return lax.dot_general(a, b, (((ca,), (cb,)), ((), ())), preferred_element_type=F32)


def flip_bits(index, mask):
    out = index
    bit = 1
    while bit <= mask:
        if mask & bit:
            out = out + bit - 2 * bit * ((index // bit) % 2)
        bit *= 2
    return out


def main_kernel(
    dims,
    off_ref, q_hbm, k_hbm, v_hbm, w_hbm, x_hbm,
    dq_hbm, dk_hbm, dv_hbm, gw_hbm,
    x, qkv, w, wt, perm, out_t, recv, res, ret, kk, vv, vt1, acc, term, part, half, pair_in, near_out, landed, cross_out, cross_in, mine,
    laid, gw,
    x_sem, in_sem, w_sem, qkv_send, qkv_recv, g_send, g_recv, res_send, ret_recv, attn_send, attn_recv,
    pair_send, pair_recv, red_send, red_recv, cross_send, cross_recv, out_sem, gw_sem,
):
    rounds, rows, width, heads, head_dim, tok, phases = dims
    seg = heads * rows
    me = lax.axis_index("tok")
    lane = me % heads
    base = me - lane
    order = sorted(range(1, heads), key=lambda s: (-(s // (heads // 2)), -s))
    across = [s for s in order if s >= heads // 2]
    within = [s for s in order if s < heads // 2]
    quarter = lane // (heads // 4)
    outer = jnp.logical_or(quarter == 0, quarter == 3)
    inner = jnp.logical_not(outer)
    scale = head_dim ** (-0.5)
    group = heads // 2
    groups = tok // group
    lo = me % group
    hi = me // group
    chip = lo // 2
    core = lo % 2
    chips = group // 2
    own = width // tok
    chunks = rows // PACK

    greet = sorted(set(range(1, heads)) | set(group * s for s in range(1, groups)))
    barrier = pltpu.get_barrier_semaphore()
    for s in greet:
        pl.semaphore_signal(barrier, inc=1, device_id={"tok": flip_bits(me, s)}, device_id_type=MESH)

    def load_qkv(r):
        return [
            pltpu.make_async_copy(ref.at[r], qkv.at[r, a], in_sem.at[r, a])
            for a, ref in enumerate((q_hbm, k_hbm, v_hbm))
        ]

    def load_x(r):
        return pltpu.make_async_copy(x_hbm.at[r], x.at[r], x_sem.at[r])

    load_w = pltpu.make_async_copy(w_hbm, w, w_sem)
    for r in range(rounds):
        for copy in load_qkv(r):
            copy.start()
        if r == 0:
            load_w.start()
        load_x(r).start()

    def columns(d):
        return pl.ds(pl.multiple_of(d * rows, rows), rows)

    def send_to(peers, r, first, count, send_sem, recv_sem):
        for s in peers:
            d = flip_bits(lane, s)
            pltpu.make_async_remote_copy(
                src_ref=out_t.at[r, pl.ds(first, count), d],
                dst_ref=recv.at[r, pl.ds(first, count), :, columns(lane)],
                send_sem=send_sem.at[r],
                recv_sem=recv_sem.at[r],
                device_id={"tok": base + d},
                device_id_type=MESH,
            ).start()

    def send_across(r, first, count, send_sem, recv_sem):
        send_to(across, r, first, count, send_sem, recv_sem)

    def send_within(r, first, count, send_sem, recv_sem):
        send_to(within, r, first, count, send_sem, recv_sem)
        pltpu.make_async_copy(
            out_t.at[r, pl.ds(first, count), lane],
            recv.at[r, pl.ds(first, count), :, columns(lane)],
            recv_sem.at[r],
        ).start()

    def turn(r):
        for a, copy in enumerate(load_qkv(r)):
            copy.wait()
            out_t[r, a] = qkv[r, a].T.reshape(heads, head_dim, rows)

    def project(r):
        load_x(r).wait()

        def chunk(c, inner):
            x[r, c] = dot(perm[...], x[r, c], 1, 0).astype(BF16)
            return inner

        lax.fori_loop(0, chunks, chunk, 0)
        for h in range(heads):
            chosen = x[r, :, h * PACK : (h + 1) * PACK, :].reshape(rows, width)
            out_t[r, 3, h] = dot(wt[h * head_dim : (h + 1) * head_dim, :], chosen, 1, 1).astype(BF16)

    at = lax.broadcasted_iota(jnp.int32, (PACK, PACK * phases), 1)
    at = at - phases * lax.broadcasted_iota(jnp.int32, (PACK, PACK * phases), 0)
    for h in range(heads):
        perm[h * PACK : (h + 1) * PACK, :] = jnp.where(at == off_ref[h], 1.0, 0.0).astype(BF16)
    for a, copy in enumerate(load_qkv(0)):
        copy.wait()
        out_t[0, a] = qkv[0, a].T.reshape(heads, head_dim, rows)
        if a == 0:
            pl.semaphore_wait(barrier, len(greet))

        @pl.when(outer)
        def _():
            send_across(0, a, 1, qkv_send, qkv_recv)

        send_within(0, a, 1, qkv_send, qkv_recv)

        @pl.when(inner)
        def _():
            send_across(0, a, 1, qkv_send, qkv_recv)

    load_w.wait()
    wt[...] = w[...].T

    def prepare(r, carry):
        project(r)

        @pl.when(jnp.logical_and(r == 0, outer))
        def _():
            send_across(r, 3, 1, g_send, g_recv)

        send_within(r, 3, 1, g_send, g_recv)

        @pl.when(inner)
        def _():
            send_across(r, 3, 1, g_send, g_recv)

        @pl.when(r + 1 < rounds)
        def _():
            turn(r + 1)
            send_within(r + 1, 0, 3, qkv_send, qkv_recv)

            @pl.when(inner)
            def _():
                send_across(r + 1, 0, 3, qkv_send, qkv_recv)

        return carry

    lax.fori_loop(0, rounds, prepare, 0)

    def send_back(r, a, send_sem, recv_sem):
        def send_to_all(peers):
            for s in peers:
                d = flip_bits(lane, s)
                pltpu.make_async_remote_copy(
                    src_ref=res.at[r, a, :, columns(d)],
                    dst_ref=ret.at[r, a, lane],
                    send_sem=send_sem,
                    recv_sem=recv_sem,
                    device_id={"tok": base + d},
                    device_id_type=MESH,
                ).start()

        @pl.when(outer)
        def _():
            send_to_all(across)

        send_to_all(within)
        pltpu.make_async_copy(res.at[r, a, :, columns(lane)], ret.at[r, a, lane], recv_sem).start()

        @pl.when(inner)
        def _():
            send_to_all(across)

    def send_attn(r):
        send_back(r, 3, attn_send.at[r], attn_recv.at[r])

    def send_grad(r, a):
        send_back(r, a, res_send.at[r, a], ret_recv.at[r, a])

    block = seg // 2
    k_pad = jnp.zeros((LANES - 2 * head_dim, seg), BF16)
    v_pad = jnp.zeros((LANES - head_dim - PACK, seg), BF16)
    ones = jnp.ones((PACK, seg), BF16)

    def attend(r, carry):
        got = recv.at[r, pl.ds(0, 3)]
        pltpu.make_async_copy(got, got, qkv_recv.at[r]).wait()
        pltpu.make_async_copy(recv.at[r, 3], recv.at[r, 3], g_recv.at[r]).wait()

        @pl.when(jnp.logical_and(outer, r + 1 < rounds))
        def _():
            send_across(r + 1, 0, 3, qkv_send, qkv_recv)
            send_across(r + 1, 3, 1, g_send, g_recv)

        @pl.when(r == rounds - 2)
        def _():
            def one(i, inner_carry):
                send_attn(i)
                return inner_carry

            lax.fori_loop(0, rounds - 2, one, 0)
            send_grad(0, 0)
            send_grad(0, 1)
            send_grad(0, 2)

        kt = recv[r, 1]
        vt = recv[r, 2]
        kk[...] = jnp.concatenate([kt, kt, k_pad], 0).T
        vv[...] = jnp.concatenate([vt, ones, v_pad], 0).T
        vt1[...] = jnp.concatenate([vt, ones], 0)
        acc[...] = jnp.zeros_like(acc)
        def q_block(b, inner):
            cols = pl.ds(pl.multiple_of(b * block, block), block)
            qt = recv[r, 0, :, cols].astype(F32)
            gt = recv[r, 3, :, cols]
            gf = gt.astype(F32)
            qc = qt * (scale * LOG2E)
            q_high = qc.astype(BF16)
            q_low = (qc - q_high.astype(F32)).astype(BF16)
            q_two = jnp.concatenate([q_high, q_low, jnp.zeros((LANES - 2 * head_dim, block), BF16)], 0)
            s = dot(kk[...], q_two, 1, 0)
            e = jnp.exp2(s - jnp.max(s, axis=0, keepdims=True)).astype(BF16)
            both = dot(vt1[...], e, 1, 0)
            inv = 1.0 / both[head_dim : head_dim + 1]
            ot = (both[:head_dim] * inv).astype(BF16)
            res[r, 3, :, cols] = ot
            minus = -jnp.sum(gf * ot.astype(F32), axis=0, keepdims=True)
            m_high = minus.astype(BF16).astype(F32)
            row = lax.broadcasted_iota(jnp.int32, (PACK, block), 0)
            m_two = jnp.where(row == 0, m_high, jnp.where(row == 1, minus - m_high, 0.0)).astype(BF16)
            g_two = jnp.concatenate([gt, m_two, jnp.zeros((LANES - head_dim - PACK, block), BF16)], 0)
            ds = e * dot(vv[...], g_two, 1, 0).astype(BF16)
            res[r, 0, :, cols] = (dot(kt, ds, 1, 0) * (inv * scale)).astype(BF16)
            qs = (qt * (inv * scale)).astype(BF16)
            gs = (gf * inv).astype(BF16)
            zero = jnp.zeros((head_dim, block), BF16)
            right = jnp.concatenate(
                [
                    jnp.concatenate([gs, zero], 1),
                    jnp.concatenate([zero, qs], 1),
                    jnp.zeros((LANES - 2 * head_dim, 2 * block), BF16),
                ],
                0,
            )
            acc[...] += dot(jnp.concatenate([e, ds], 1), right, 1, 1)
            return inner

        lax.fori_loop(0, seg // block, q_block, 0)

        @pl.when(r >= rounds - 2)
        def _():
            send_attn(r)

        t = acc[...].astype(BF16).T
        res[r, 2] = t[:head_dim]
        res[r, 1] = t[head_dim : 2 * head_dim]

        @pl.when(r == rounds - 2)
        def _():
            send_grad(1, 0)
            send_grad(1, 1)

        return carry

    lax.fori_loop(0, rounds, attend, 0)
    later = [(r, a) for r in range(rounds) for a in range(3)][5:]
    for piece in later[:2]:
        send_grad(*piece)

    term[...] = jnp.zeros_like(term)

    def finish(r, carry):
        pltpu.make_async_copy(ret.at[r, 3], ret.at[r, 3], attn_recv.at[r]).wait()
        for h in range(heads):
            chosen = x[r, :, h * PACK : (h + 1) * PACK, :].reshape(rows, width)
            here = pl.ds(h * head_dim, head_dim)
            term[here, :] += dot(ret[r, 3, h], chosen, 1, 0)
        return carry

    lax.fori_loop(0, rounds, finish, 0)
    part[...] = term[...].T.reshape(groups, chips, 2, own, width)
    half[...] = part[...].astype(BF16)
    pair = pltpu.make_async_remote_copy(
        src_ref=half.at[:, :, 1 - core],
        dst_ref=pair_in,
        send_sem=pair_send,
        recv_sem=pair_recv,
        device_id={"tok": me + 1 - 2 * core},
        device_id_type=MESH,
    )

    def near(s):
        return pltpu.make_async_remote_copy(
            src_ref=near_out.at[:, flip_bits(chip, s)],
            dst_ref=landed.at[chip],
            send_sem=red_send.at[s],
            recv_sem=red_recv.at[s],
            device_id={"tok": hi * group + flip_bits(chip, s) * 2 + core},
            device_id_type=MESH,
        )

    def far(s):
        return pltpu.make_async_remote_copy(
            src_ref=cross_out.at[flip_bits(hi, s)],
            dst_ref=cross_in.at[hi],
            send_sem=cross_send.at[s],
            recv_sem=cross_recv.at[s],
            device_id={"tok": flip_bits(hi, s) * group + lo},
            device_id_type=MESH,
        )

    def lay_out(r):
        for a, ref in enumerate((dq_hbm, dk_hbm, dv_hbm)):
            pltpu.make_async_copy(ret.at[r, a], ret.at[r, a], ret_recv.at[r, a]).wait()
            laid[r, a] = ret[r, a].reshape(width, rows).T
            pltpu.make_async_copy(laid.at[r, a], ref.at[r], out_sem.at[r, a]).start()

    pair.start()
    for piece in later[2:5]:
        send_grad(*piece)
    pair.wait()
    for j in range(groups):
        for u in range(chips):
            near_out[j, u] = (part[j, u, core] + pair_in[j, u].astype(F32)).astype(BF16)
        mine[j] = part[j, chip, core] + pair_in[j, chip].astype(F32)
    beside = later[5:7]
    for s in range(1, chips):
        near(s).start()
        for piece in beside[(s - 1) * len(beside) // (chips - 1) : s * len(beside) // (chips - 1)]:
            send_grad(*piece)
    for piece in later[7:7]:
        send_grad(*piece)
    lay_out(0)
    for s in range(1, chips):
        near(s).wait()
    for j in range(groups):
        total = mine[j]
        for s in range(1, chips):
            total = total + landed[flip_bits(chip, s), j].astype(F32)
        mine[j] = total
        cross_out[j] = total.astype(BF16)
    for s in range(1, groups):
        far(s).start()
    for piece in later[7:]:
        send_grad(*piece)
    for r in range(1, rounds - 1):
        lay_out(r)
    lay_out(rounds - 1)
    for s in range(1, groups):
        far(s).wait()
    total = mine[hi]
    for s in range(1, groups):
        total = total + cross_in[flip_bits(hi, s)].astype(F32)
    gw[...] = total
    pltpu.make_async_copy(gw, gw_hbm, gw_sem).start()

    for r in range(rounds):
        blocks = pl.ds(0, heads - 1)
        sent = out_t.at[r, pl.ds(0, 3), blocks]
        pltpu.make_async_copy(sent, sent, qkv_send.at[r]).wait()
        sent = out_t.at[r, 3, blocks]
        pltpu.make_async_copy(sent, sent, g_send.at[r]).wait()
        for a in range(3):
            sent = ret.at[r, a, blocks]
            pltpu.make_async_copy(sent, sent, res_send.at[r, a]).wait()
        sent = ret.at[r, 3, blocks]
        pltpu.make_async_copy(sent, sent, attn_send.at[r]).wait()
    for r in range(rounds):
        for a, ref in enumerate((dq_hbm, dk_hbm, dv_hbm)):
            pltpu.make_async_copy(laid.at[r, a], ref.at[r], out_sem.at[r, a]).wait()
    pltpu.make_async_copy(gw, gw_hbm, gw_sem).wait()


def hand_over(*refs):
    count = (len(refs) - 2) // 3
    got, given, kept = refs[:count], refs[count : 2 * count], refs[2 * count : 3 * count]
    in_sem, out_sem = refs[3 * count :]
    pieces = [(i, r) for r in range(got[0].shape[0]) for i in range(count - 1)] + [(count - 1, None)]

    def both(n, i, r):
        a, b, c = (got[i], given[i], kept[i]) if r is None else (got[i].at[r], given[i].at[r], kept[i].at[r])
        return pltpu.make_async_copy(a, c, in_sem.at[n]), pltpu.make_async_copy(c, b, out_sem.at[n])

    copies = [both(n, i, r) for n, (i, r) in enumerate(pieces)]
    for into, _ in copies:
        into.start()
    for into, out_of in copies:
        into.wait()
        out_of.start()
    for _, out_of in copies:
        out_of.wait()


def local(queries, key_rows, value_rows, projected_output_gradient, out_weight, offsets):
    rounds, rows, width = queries.shape
    heads = offsets.shape[0]
    head_dim = width // heads
    tok = lax.axis_size("tok")
    phases = projected_output_gradient.shape[1] // rows
    seg = heads * rows
    own = width // tok
    group = heads // 2
    groups = tok // group
    dims = (rounds, rows, width, heads, head_dim, tok, phases)
    tokens = projected_output_gradient.reshape(rounds, rows // PACK, PACK * phases, width)
    hbm = pl.BlockSpec(memory_space=pl.ANY)
    rows_shape = jax.ShapeDtypeStruct((rounds, rows, width), BF16)
    out_shape = (rows_shape, rows_shape, rows_shape, jax.ShapeDtypeStruct((own, width), F32))
    dma = pltpu.SemaphoreType.DMA
    results = pl.pallas_call(
        functools.partial(main_kernel, dims),
        out_shape=out_shape,
        in_specs=[pl.BlockSpec(memory_space=pltpu.SMEM)] + [hbm] * 5,
        out_specs=(hbm,) * 4,
        scratch_shapes=[
            pltpu.VMEM((rounds, rows // PACK, PACK * phases, width), BF16),
            pltpu.VMEM((rounds, 3, rows, width), BF16),
            pltpu.VMEM((width, width), BF16),
            pltpu.VMEM((width, width), BF16),
            pltpu.VMEM((PACK * heads, PACK * phases), BF16),
            pltpu.VMEM((rounds, 4, heads, head_dim, rows), BF16),
            pltpu.VMEM((rounds, 4, head_dim, seg), BF16),
            pltpu.VMEM((rounds, 4, head_dim, seg), BF16),
            pltpu.VMEM((rounds, 4, heads, head_dim, rows), BF16),
            pltpu.VMEM((seg, LANES), BF16),
            pltpu.VMEM((seg, LANES), BF16),
            pltpu.VMEM((head_dim + PACK, seg), BF16),
            pltpu.VMEM((seg, LANES), F32),
            pltpu.VMEM((width, width), F32),
            pltpu.VMEM((groups, group // 2, 2, own, width), F32),
            pltpu.VMEM((groups, group // 2, 2, own, width), BF16),
            pltpu.VMEM((groups, group // 2, own, width), BF16),
            pltpu.VMEM((groups, group // 2, own, width), BF16),
            pltpu.VMEM((group // 2, groups, own, width), BF16),
            pltpu.VMEM((groups, own, width), BF16),
            pltpu.VMEM((groups, own, width), BF16),
            pltpu.VMEM((groups, own, width), F32),
            pltpu.VMEM((rounds, 3, rows, width), BF16),
            pltpu.VMEM((own, width), F32),
            dma((rounds,)),
            dma((rounds, 3)),
            dma,
            dma((rounds,)),
            dma((rounds,)),
            dma((rounds,)),
            dma((rounds,)),
            dma((rounds, 3)),
            dma((rounds, 3)),
            dma((rounds,)),
            dma((rounds,)),
            dma,
            dma,
            dma((group // 2,)),
            dma((group // 2,)),
            dma((groups,)),
            dma((groups,)),
            dma((rounds, 3)),
            dma,
        ],
        compiler_params=pltpu.CompilerParams(
            collective_id=0, has_side_effects=True, vmem_limit_bytes=66000000
        ),
        name="branch_backward",
    )(offsets, queries, key_rows, value_rows, out_weight, tokens)
    return pl.pallas_call(
        hand_over,
        out_shape=out_shape,
        in_specs=[hbm] * 4,
        out_specs=(hbm,) * 4,
        scratch_shapes=[pltpu.VMEM(a.shape, a.dtype) for a in out_shape] + [dma((3 * rounds + 1,)), dma((3 * rounds + 1,))],
        name="hand_over",
    )(*results)


def solution(mesh):
    placed = (
        P("slides", "tok", None),
        P("slides", "tok", None),
        P("slides", "tok", None),
        P("slides", "tok", None),
        P(),
        P(),
    )
    return jax.shard_map(
        local,
        mesh=mesh,
        in_specs=placed,
        out_specs=(
            P("slides", "tok", None),
            P("slides", "tok", None),
            P("slides", "tok", None),
            P(("slides", "tok"), None),
        ),
        check_vma=False,
    )
```
